256 devices in a mesh: slab: 32 (over z, y), snap: 8 (over x, core).
Axes of the slice: x: 4, y: 4, z: 8, core: 2. Of those that a mesh axis runs over, the one named last changes fastest.
Arguments:
- flow: bfloat16 [128, 3, 64, 64, 128], P('snap', None, 'slab'), may hold values from -127 to 127
- large_scale: bfloat16 [3, 64, 64, 128], P(None, 'slab'), may hold values from -6 to 6
- modulation: float32 [128, 64], replicated, may hold values from -15 to 15
- metric: float32 [4, 64, 64, 128], P(None, 'slab'), may hold values from -0.5 to 9.6
Outputs:
- whitened: float32 [128, 3, 64, 64, 128], P(None, None, 'slab', 'snap')
The draws below stay inside these ranges and needn't reach their ends.
All inputs are finite; a program needn't handle non-finite values.
Results may differ from the reference program's by a relative error of at most 0.0003.
Values may be sent and summed in bfloat16 or wider, within the bound.
A program may use at most 64 MiB of HBM per device.

```python
import math
import jax
import jax.numpy as jnp
from jax import lax

NX = 64
NZ = 128
NSITER = 6
S = 128
NY = 64


def draw_flow(key, part):
    key_base, key_snap, key_plane = jax.random.split(key, 3)
    shape_all = (S, 3, NY, NX, NZ)
    base = jax.random.truncated_normal(key_base, -4.0, 4.0, shape_all, jnp.float32)
    snap_scale = jnp.exp(jax.random.uniform(key_snap, (S,), jnp.float32) * math.log(10.0))
    plane_scale = jnp.exp(jax.random.uniform(key_plane, (NY,), jnp.float32) * (0.5 * math.log(10.0)))
    values = base * snap_scale[:, None, None, None, None] * plane_scale[None, None, :, None, None]
    return values.astype(jnp.bfloat16)


def draw_metric(key, part):
    key_x, key_shear, key_y, key_z = jax.random.split(key, 4)
    shape_cells = (NY, NX, NZ)
    planes_pos = jnp.arange(NY).astype(jnp.float32) / max(NY - 1, 1)
    stretch = 1.0 + 3.0 * planes_pos
    metric_x = jax.random.uniform(key_x, shape_cells, jnp.float32, 0.6, 1.6)
    shear_xy = jax.random.uniform(key_shear, shape_cells, jnp.float32, -0.5, 0.5)
    metric_y = stretch[:, None, None] * jax.random.uniform(key_y, shape_cells, jnp.float32, 0.6, 1.6)
    metric_z = jax.random.uniform(key_z, shape_cells, jnp.float32, 0.6, 1.6)
    return jnp.stack([metric_x, shear_xy, metric_y, metric_z], axis=0)


def shard_levels(key, shape, cuts, smallest, high):
    def one(position, shards_of):
        draws = jax.random.uniform(jax.random.fold_in(jax.random.fold_in(key, 6), position), (shards_of,), jnp.float32, smallest / len(cuts), high / len(cuts))
        return jnp.repeat(jnp.exp(draws), shape[position] // shards_of).reshape((-1,) + (1,) * (len(shape) - position - 1))

    level = one(*cuts[0])
    for cut in cuts[1:]:
        level = level * one(*cut)
    return level


def gaussian(key, shape, width, limit, cuts=(), kind=jnp.bfloat16):
    factor_of = shard_levels(key, shape, cuts, -0.22, 0.18) if cuts else 1.0
    array = jax.random.normal(key, shape, jnp.float32) * width * factor_of
    return jnp.minimum(jnp.maximum(array, -limit), limit).astype(kind)


def setup_inputs(seed: int = 0) -> dict:
    seeds = jax.random.split(jax.random.key(seed), 5)
    flow = draw_flow(jax.random.fold_in(seeds[4], 71), 0)
    large_scale = gaussian(seeds[1], (3, NY, NX, NZ), 1.0, 6.0, ((1, 32),))
    modulation = gaussian(seeds[2], (S, NX), 3.0, 15.0, (), jnp.float32)
    metric = draw_metric(jax.random.fold_in(seeds[4], 71), 0)
    return {"flow": flow, "large_scale": large_scale, "modulation": modulation, "metric": metric}


def vorticity(velocity, metric):
    metric_x = metric[0]
    shear_xy = metric[1]
    metric_y = metric[2]
    metric_z = metric[3]

    def along_x(values):
        return 0.5 * (values[..., 1:-1, 2:, :] - values[..., 1:-1, :-2, :])

    def along_y(values):
        return 0.5 * (values[..., 2:, 1:-1, :] - values[..., :-2, 1:-1, :])

    def along_z(values):
        center = values[..., 1:-1, 1:-1, :]
        return 0.5 * (jnp.roll(center, -1, -1) - jnp.roll(center, 1, -1))

    def slope_x(values):
        return metric_x * along_x(values) + shear_xy * along_y(values)

    def slope_y(values):
        return metric_y * along_y(values)

    def slope_z(values):
        return metric_z * along_z(values)
    stream = velocity[..., 0, :, :, :]
    normal = velocity[..., 1, :, :, :]
    spanwise = velocity[..., 2, :, :, :]
    around_x = slope_y(spanwise) - slope_z(normal)
    around_y = slope_z(stream) - slope_x(spanwise)
    around_z = slope_x(normal) - slope_y(stream)
    return jnp.stack([around_x, around_y, around_z], axis=-4)

def wrap_columns(values):
    return jnp.concatenate([values[..., -1:, :], values, values[..., :1, :]], axis=-2)

def whitening(correlation):
    identity = jnp.eye(correlation.shape[0], dtype=correlation.dtype)
    frob_scale = jnp.sqrt(jnp.sum(correlation * correlation) + 1e-06)
    approx = correlation / frob_scale
    inverse = identity
    for repeat in range(NSITER):
        factor = 0.5 * (3.0 * identity - jnp.dot(inverse, approx, precision=lax.Precision.HIGHEST))
        approx = jnp.dot(approx, factor, precision=lax.Precision.HIGHEST)
        inverse = jnp.dot(factor, inverse, precision=lax.Precision.HIGHEST)
    return inverse / jnp.sqrt(frob_scale)

def reference(flow, large_scale, modulation, metric):
    large_field = large_scale.astype(jnp.float32)

    def single(inputs):
        snapshot, amplitude = inputs
        velocity = snapshot.astype(jnp.float32) + amplitude[None, None, :, None] * large_field
        padded = jnp.pad(velocity, ((0, 0), (1, 1), (0, 0), (0, 0)))
        return vorticity(wrap_columns(padded), metric)
    fields = lax.map(single, (flow, modulation))
    snapshot_rows = fields.reshape(fields.shape[0], -1)
    gram_total = lax.dot_general(snapshot_rows, snapshot_rows, (((1,), (1,)), ((), ())), precision=lax.Precision.HIGHEST, preferred_element_type=jnp.float32)
    correlation = gram_total / snapshot_rows.shape[1]
    weights = whitening(correlation)
    result = jnp.dot(weights, snapshot_rows, precision=lax.Precision.HIGHEST)
    return result.reshape(fields.shape)
```

```python
import functools

import jax
import jax.numpy as jnp
from jax import lax
from jax.experimental import pallas as pl
from jax.experimental.pallas import tpu as pltpu
from jax.sharding import PartitionSpec as P

NSITER = 6
F32 = jnp.float32
BF16 = jnp.bfloat16
MESH = pl.DeviceIdType.MESH


def remote(src, dst, ssem, rsem, dev):
    return pltpu.make_async_remote_copy(
        src_ref=src, dst_ref=dst, send_sem=ssem, recv_sem=rsem, device_id=dev, device_id_type=MESH
    )


def wait_bytes(ref, sem):
    pltpu.make_async_copy(ref, ref, sem).wait()


def gather_kernel(
    flow_hbm, large_hbm, mod_hbm, metric_hbm,
    vh_hbm, vl_hbm, g_out,
    flow_v, flow_f, send, cols, halo, large_b, large_f, mod_v, mod_b, met,
    vh, vl, acc, gs, rx, ys, ry, zs, rz, ag, gf,
    in_sem, big_sem, xs_sem, xr_sem, hs_sem, hr_sem, ls_sem, lr_sem, v_sem, as_sem, ar_sem,
):
    slab = lax.axis_index("slab")
    i = lax.axis_index("snap")
    z = slab // 4
    y = lax.rem(slab, 4)
    up = lax.rem(slab + 1, 32)
    down = lax.rem(slab + 31, 32)

    flow_in = pltpu.make_async_copy(flow_hbm, flow_v, big_sem)
    flow_in.start()
    large_in = pltpu.make_async_copy(large_hbm, large_b, in_sem.at[0])
    large_in.start()
    mod_in = pltpu.make_async_copy(mod_hbm, mod_v, in_sem.at[1])
    mod_in.start()
    met_in = pltpu.make_async_copy(
        metric_hbm.at[:, :, pl.ds(pl.multiple_of(8 * i, 8), 8), :], met, in_sem.at[2]
    )
    met_in.start()

    snap_dev = [{"slab": slab, "snap": lax.rem(i + d, 8)} for d in range(1, 8)]
    y_dev = [{"slab": z * 4 + lax.rem(y + d, 4), "snap": i} for d in range(1, 4)]
    z_dev = [{"slab": lax.rem(z + d, 8) * 4 + y, "snap": i} for d in range(1, 8)]
    side_dev = [{"slab": down, "snap": i}, {"slab": up, "snap": i}]
    barrier = pltpu.get_barrier_semaphore()
    everyone = snap_dev + y_dev + z_dev + side_dev
    for dev in everyone:
        pl.semaphore_signal(barrier, inc=1, device_id=dev, device_id_type=MESH)

    large_in.wait()
    for c in range(3):
        for p in range(2):
            large_f[c, p + 1] = large_b[c, p].astype(F32)
    flow_in.wait()

    def widen(s, carry):
        flow_f[pl.ds(pl.multiple_of(s * 384, 384), 384), :] = flow_v[s].astype(F32)
        return carry

    lax.fori_loop(0, 16, widen, 0)

    def transpose(t):
        for b in range(8):
            for cy in range(6):
                tile = flow_f[pl.ds(cy * 64 + 8 * b + t, 16, stride=384), :]
                send[8 * b + t, cy // 2, cy % 2] = tile.astype(BF16)

    transpose(0)
    pl.semaphore_wait(barrier, len(everyone))

    mine16 = pl.ds(pl.multiple_of(16 * i, 16), 16)
    rows8 = pl.ds(pl.multiple_of(8 * i, 8), 8)
    large_copies = [
        remote(large_f.at[:, 1, rows8, :], large_f.at[:, 3, rows8, :], ls_sem.at[0], lr_sem.at[0], side_dev[0]),
        remote(large_f.at[:, 2, rows8, :], large_f.at[:, 0, rows8, :], ls_sem.at[1], lr_sem.at[1], side_dev[1]),
    ]
    for copy in large_copies:
        copy.start()

    def send_step(t, carry):
        @pl.when(t < 7)
        def _():
            transpose(t + 1)

        for d in range(1, 8):
            target = lax.rem(i + d, 8)
            remote(
                send.at[8 * target + t], cols.at[t + 1, :, :, mine16, :],
                xs_sem.at[t + 1], xr_sem.at[t + 1], {"slab": slab, "snap": target},
            ).start()
        pltpu.make_async_copy(
            send.at[8 * i + t], cols.at[t + 1, :, :, mine16, :], xr_sem.at[t + 1]
        ).start()
        return carry

    lax.fori_loop(0, 8, send_step, 0)
    for slot, shift in ((0, 63), (9, 8)):
        for d in range(1, 8):
            target = lax.rem(i + d, 8)
            remote(
                send.at[lax.rem(8 * target + shift, 64), pl.ds(1, 2)],
                cols.at[slot, pl.ds(1, 2), :, mine16, :],
                xs_sem.at[slot], xr_sem.at[slot], {"slab": slab, "snap": target},
            ).start()
        pltpu.make_async_copy(
            send.at[lax.rem(8 * i + shift, 64), pl.ds(1, 2)],
            cols.at[slot, pl.ds(1, 2), :, mine16, :], xr_sem.at[slot],
        ).start()

    mod_in.wait()

    def spread(k, carry):
        column = lax.rem(8 * i + k + 63, 64)
        mod_b[k] = jnp.broadcast_to(mod_v[pl.ds(column, 1), :], (128, 128)).T
        return carry

    lax.fori_loop(0, 10, spread, 0)
    met_in.wait()
    for copy in large_copies:
        copy.wait()

    @pl.when(slab == 0)
    def _():
        large_f[:, 0] = jnp.zeros((3, 64, 128), F32)

    @pl.when(slab == 31)
    def _():
        large_f[:, 3] = jnp.zeros((3, 64, 128), F32)

    acc[...] = jnp.zeros((128, 256), F32)

    def pass_on(xx):
        wait_bytes(cols.at[xx], xr_sem.at[xx])
        for side in range(2):
            remote(
                cols.at[xx, :, side], halo.at[1 - side, xx - 1],
                hs_sem.at[side, xx - 1], hr_sem.at[1 - side, xx - 1], side_dev[side],
            ).start()

    def pass_step(k, carry):
        pass_on(k + 1)
        return carry

    lax.fori_loop(0, 3, pass_step, 0)

    def write_out(xx):
        lanes = pl.ds(pl.multiple_of(128 * (xx - 1), 128), 128)
        pltpu.make_async_copy(vh.at[:, :, lanes], vh_hbm.at[:, :, lanes], v_sem.at[0]).start()
        pltpu.make_async_copy(vl.at[:, :, lanes], vl_hbm.at[:, :, lanes], v_sem.at[1]).start()

    def column(k, carry):
        xx = lax.rem(k + 1, 8) + 1

        @pl.when(k < 5)
        def _():
            pass_on(k + 4)

        @pl.when(k == 6)
        def _():
            wait_bytes(cols.at[0, pl.ds(1, 2)], xr_sem.at[0])
            wait_bytes(cols.at[9, pl.ds(1, 2)], xr_sem.at[9])

        for side in range(2):
            wait_bytes(halo.at[side, xx - 1], hr_sem.at[side, xx - 1])

        @pl.when(slab == 0)
        def _():
            halo[0, xx - 1] = jnp.zeros((3, 128, 128), BF16)

        @pl.when(slab == 31)
        def _():
            halo[1, xx - 1] = jnp.zeros((3, 128, 128), BF16)

        here = 8 * i + xx - 1
        before = lax.rem(here + 63, 64)
        after = lax.rem(here + 1, 64)
        base = [[large_f[c, p, pl.ds(here, 1), :] for p in range(4)] for c in range(3)]
        base_m = [[large_f[c, p + 1, pl.ds(before, 1), :] for p in range(2)] for c in (1, 2)]
        base_p = [[large_f[c, p + 1, pl.ds(after, 1), :] for p in range(2)] for c in (1, 2)]
        half = [[0.5 * met[m, p, pl.ds(xx - 1, 1), :] for p in range(2)] for m in range(4)]
        lanes = pl.ds(pl.multiple_of(128 * (xx - 1), 128), 128)

        def snaps(s, inner):
            r = pl.ds(pl.multiple_of(16 * s, 16), 16)
            m0 = mod_b[xx, r, :]
            mm = mod_b[xx - 1, r, :]
            mp = mod_b[xx + 1, r, :]

            def field(c):
                return [
                    halo[0, xx - 1, c, r, :].astype(F32) + m0 * base[c][0],
                    cols[xx, c, 0, r, :].astype(F32) + m0 * base[c][1],
                    cols[xx, c, 1, r, :].astype(F32) + m0 * base[c][2],
                    halo[1, xx - 1, c, r, :].astype(F32) + m0 * base[c][3],
                ]

            def along_x(c, p):
                right = cols[xx + 1, c, p, r, :].astype(F32) + mp * base_p[c - 1][p]
                left = cols[xx - 1, c, p, r, :].astype(F32) + mm * base_m[c - 1][p]
                return right - left

            def along_z(f):
                return pltpu.roll(f, 127, 1) - pltpu.roll(f, 1, 1)

            u, v, w = field(0), field(1), field(2)
            for p in range(2):
                gx, sxy, gy, gz = (half[m][p] for m in range(4))
                du = u[p + 2] - u[p]
                dv = v[p + 2] - v[p]
                dw = w[p + 2] - w[p]
                around = (
                    gy * dw - gz * along_z(v[p + 1]),
                    gz * along_z(u[p + 1]) - (gx * along_x(2, p) + sxy * dw),
                    (gx * along_x(1, p) + sxy * dv) - gy * du,
                )
                for c in range(3):
                    high = around[c].astype(BF16)
                    vh[2 * c + p, r, lanes] = high
                    vl[2 * c + p, r, lanes] = (around[c] - high.astype(F32)).astype(BF16)
            return inner

        lax.fori_loop(0, 8, snaps, 0)
        rows_h = jnp.concatenate([vh[cy, :, lanes] for cy in range(6)], axis=1)
        rows_l = jnp.concatenate([vl[cy, :, lanes] for cy in range(6)], axis=1)
        both = jnp.concatenate([rows_h, rows_l], axis=0)
        acc[...] += lax.dot_general(
            rows_h, both, (((1,), (1,)), ((), ())), preferred_element_type=F32
        )
        write_out(xx)
        return carry

    lax.fori_loop(0, 8, column, 0)
    gs[...] = 0.5 * acc[:, :128] + acc[:, 128:]

    def exchange(stage, src_of, dst, slot, devs, ids, width):
        for dev, target in zip(devs, ids):
            remote(src_of(target), dst.at[slot], as_sem.at[stage], ar_sem.at[stage], dev).start()
        pltpu.make_async_copy(src_of(slot_id[stage]), dst.at[slot], ar_sem.at[stage]).start()
        wait_bytes(dst, ar_sem.at[stage])

    slot_id = {0: i, 1: y, 2: z, 3: i}
    snap_ids = [lax.rem(i + d, 8) for d in range(1, 8)]

    def rows_of(k):
        return gs.at[pl.ds(pl.multiple_of(16 * k, 16), 16)]

    exchange(0, rows_of, rx, i, snap_dev, snap_ids, 8)
    ys[...] = jnp.sum(rx[...], axis=0)
    exchange(1, lambda k: ys, ry, y, y_dev, [None] * 3, 4)
    zs[...] = jnp.sum(ry[...], axis=0)
    exchange(2, lambda k: zs, rz, z, z_dev, [None] * 7, 8)
    ag[...] = jnp.sum(rz[...], axis=0)
    exchange(3, lambda k: ag, gf, i, snap_dev, [None] * 7, 8)
    g_out[...] = gf[...]

    for t in range(8):
        wait_bytes(send.at[pl.ds(0, 7)], xs_sem.at[t + 1])
    for slot in (0, 9):
        wait_bytes(send.at[pl.ds(0, 7), pl.ds(1, 2)], xs_sem.at[slot])
    for side in range(2):
        for k in range(8):
            wait_bytes(cols.at[k + 1, :, side], hs_sem.at[side, k])
    pltpu.make_async_copy(vh, vh_hbm, v_sem.at[0]).wait()
    pltpu.make_async_copy(vl, vl_hbm, v_sem.at[1]).wait()
    wait_bytes(rx.at[pl.ds(0, 7)], as_sem.at[0])
    wait_bytes(ry.at[pl.ds(0, 3)], as_sem.at[1])
    wait_bytes(rz.at[pl.ds(0, 7)], as_sem.at[2])
    wait_bytes(gf.at[pl.ds(0, 7)], as_sem.at[3])


def gather(flow, large, mod_t, metric):
    any_space = pl.BlockSpec(memory_space=pl.ANY)
    dma = pltpu.SemaphoreType.DMA
    return pl.pallas_call(
        gather_kernel,
        name="gather",
        out_shape=(
            jax.ShapeDtypeStruct((6, 128, 1024), BF16),
            jax.ShapeDtypeStruct((6, 128, 1024), BF16),
            jax.ShapeDtypeStruct((8, 16, 128), F32),
        ),
        in_specs=[any_space] * 4,
        out_specs=(any_space, any_space, pl.BlockSpec(memory_space=pltpu.VMEM)),
        scratch_shapes=[
            pltpu.VMEM((16, 384, 128), BF16),
            pltpu.VMEM((6144, 128), F32),
            pltpu.VMEM((64, 3, 2, 16, 128), BF16),
            pltpu.VMEM((10, 3, 2, 128, 128), BF16),
            pltpu.VMEM((2, 8, 3, 128, 128), BF16),
            pltpu.VMEM((3, 2, 64, 128), BF16),
            pltpu.VMEM((3, 4, 64, 128), F32),
            pltpu.VMEM((64, 128), F32),
            pltpu.VMEM((10, 128, 128), F32),
            pltpu.VMEM((4, 2, 8, 128), F32),
            pltpu.VMEM((6, 128, 1024), BF16),
            pltpu.VMEM((6, 128, 1024), BF16),
            pltpu.VMEM((128, 256), F32),
            pltpu.VMEM((128, 128), F32),
            pltpu.VMEM((8, 16, 128), F32),
            pltpu.VMEM((16, 128), F32),
            pltpu.VMEM((4, 16, 128), F32),
            pltpu.VMEM((16, 128), F32),
            pltpu.VMEM((8, 16, 128), F32),
            pltpu.VMEM((16, 128), F32),
            pltpu.VMEM((8, 16, 128), F32),
            dma((3,)), dma, dma((10,)), dma((10,)), dma((2, 8)), dma((2, 8)),
            dma((2,)), dma((2,)), dma((2,)), dma((4,)), dma((4,)),
        ],
        compiler_params=pltpu.CompilerParams(collective_id=0, has_side_effects=True),
    )(flow, large, mod_t, metric)


def whiten_kernel(cells, vh_hbm, vl_hbm, g_ref, out_hbm, vh, vl, out_v, in_sem, out_sem):
    loads = [
        [
            pltpu.make_async_copy(vh_hbm.at[k], vh.at[k], in_sem.at[0, k]),
            pltpu.make_async_copy(vl_hbm.at[k], vl.at[k], in_sem.at[1, k]),
        ]
        for k in range(6)
    ]
    for pair in loads:
        for copy in pair:
            copy.start()

    half = g_ref[...]
    correlation = (half + half.T) / cells
    eye = (
        lax.broadcasted_iota(jnp.int32, (128, 128), 0) == lax.broadcasted_iota(jnp.int32, (128, 128), 1)
    ).astype(F32)
    frob_scale = jnp.sqrt(jnp.sum(correlation * correlation, keepdims=True) + 1e-06)
    dot = functools.partial(jnp.dot, precision=lax.Precision.HIGHEST, preferred_element_type=F32)
    approx = correlation / frob_scale
    factor = 0.5 * (3.0 * eye - approx)
    approx = dot(approx, factor)
    inverse = factor
    for repeat in range(1, NSITER):
        factor = 0.5 * (3.0 * eye - dot(inverse, approx))
        if repeat < NSITER - 1:
            approx = dot(approx, factor)
        inverse = dot(factor, inverse)
    weights = inverse / jnp.sqrt(frob_scale)
    w_high = weights.astype(BF16)
    w_low = (weights - w_high.astype(F32)).astype(BF16)

    stores = []
    for k in range(6):
        for copy in loads[k]:
            copy.wait()
        high = vh[k]
        result = jnp.dot(w_high, high, preferred_element_type=F32)
        result += jnp.dot(w_high, vl[k], preferred_element_type=F32)
        result += jnp.dot(w_low, high, preferred_element_type=F32)
        for x in range(8):
            out_v[k, pl.ds(x, 128, stride=8), :] = result[:, 128 * x : 128 * (x + 1)]
        store = pltpu.make_async_copy(
            out_v.at[k].reshape(128, 8, 128), out_hbm.at[:, k // 2, k % 2], out_sem.at[k]
        )
        store.start()
        stores.append(store)
    for store in stores:
        store.wait()


def whiten(vh, vl, gram, cells):
    any_space = pl.BlockSpec(memory_space=pl.ANY)
    dma = pltpu.SemaphoreType.DMA
    return pl.pallas_call(
        functools.partial(whiten_kernel, cells),
        name="whiten",
        out_shape=jax.ShapeDtypeStruct((128, 3, 2, 8, 128), F32),
        in_specs=[any_space, any_space, pl.BlockSpec(memory_space=pltpu.VMEM)],
        out_specs=any_space,
        scratch_shapes=[
            pltpu.VMEM((6, 128, 1024), BF16),
            pltpu.VMEM((6, 128, 1024), BF16),
            pltpu.VMEM((6, 1024, 128), F32),
            dma((2, 6)),
            dma((6,)),
        ],
    )(vh, vl, gram)


def per_device(flow, large_scale, modulation, metric):
    vh, vl, gram = gather(flow.reshape(16, 384, 128), large_scale, modulation.T, metric)
    return whiten(vh, vl, gram.reshape(128, 128), 3.0 * 64 * 64 * 128)


def solution(mesh):
    return jax.shard_map(
        per_device,
        mesh=mesh,
        in_specs=(
            P("snap", None, "slab", None, None),
            P(None, "slab", None, None),
            P(),
            P(None, "slab", None, None),
        ),
        out_specs=P(None, None, "slab", "snap", None),
        check_vma=False,
    )
```

```python
import functools

import jax
import jax.numpy as jnp
from jax import lax
from jax.experimental import pallas as pl
from jax.experimental.pallas import tpu as pltpu
from jax.sharding import PartitionSpec as P

NSITER = 6
F32 = jnp.float32
BF16 = jnp.bfloat16
MESH = pl.DeviceIdType.MESH


def remote(src, dst, ssem, rsem, dev):
    return pltpu.make_async_remote_copy(
        src_ref=src, dst_ref=dst, send_sem=ssem, recv_sem=rsem, device_id=dev, device_id_type=MESH
    )


def wait_bytes(ref, sem):
    pltpu.make_async_copy(ref, ref, sem).wait()


def gather_kernel(
    flow_hbm, large_hbm, mod_hbm, metric_hbm,
    vh, vl, g_out,
    flow_v, flow_f, send, cols, halo, large_b, large_f, mod_v, mod_b, met,
    acc, gs, rx, zs, rz, ag, gf,
    in_sem, big_sem, xs_sem, xr_sem, hs_sem, hr_sem, ls_sem, lr_sem, as_sem, ar_sem,
):
    slab = lax.axis_index("slab")
    i = lax.axis_index("snap")
    z = slab // 4
    y = lax.rem(slab, 4)
    up = lax.rem(slab + 1, 32)
    down = lax.rem(slab + 31, 32)

    flow_in = pltpu.make_async_copy(flow_hbm, flow_v, big_sem)
    flow_in.start()
    large_in = pltpu.make_async_copy(large_hbm, large_b, in_sem.at[0])
    large_in.start()
    mod_in = pltpu.make_async_copy(mod_hbm, mod_v, in_sem.at[1])
    mod_in.start()
    met_in = pltpu.make_async_copy(
        metric_hbm.at[:, :, pl.ds(pl.multiple_of(8 * i, 8), 8), :], met, in_sem.at[2]
    )
    met_in.start()

    q = 8 * y + i

    def plane_dev(k):
        return {"slab": z * 4 + k // 8, "snap": lax.rem(k, 8)}

    def column_dev(k):
        return {"slab": k * 4 + y, "snap": i}

    side_dev = [{"slab": down, "snap": i}, {"slab": up, "snap": i}]
    barrier = pltpu.get_barrier_semaphore()

    def greet(dev):
        pl.semaphore_signal(barrier, inc=1, device_id=dev, device_id_type=MESH)

    def greet_plane(d, carry):
        greet(plane_dev(lax.rem(q + d, 32)))
        return carry

    def greet_column(d, carry):
        greet(column_dev(lax.rem(z + d, 8)))
        return carry

    lax.fori_loop(1, 8, greet_column, 0)
    lax.fori_loop(1, 32, greet_plane, 0)
    for dev in side_dev:
        greet(dev)

    large_in.wait()
    for c in range(3):
        for p in range(2):
            large_f[c, p + 1] = large_b[c, p].astype(F32)
    flow_in.wait()

    def widen(s, carry):
        flow_f[pl.ds(pl.multiple_of(s * 384, 384), 384), :] = flow_v[s].astype(F32)
        return carry

    lax.fori_loop(0, 16, widen, 0)

    def transpose(t):
        for b in range(8):
            for cy in range(6):
                tile = flow_f[pl.ds(cy * 64 + 8 * b + t, 16, stride=384), :]
                send[8 * b + t, cy // 2, cy % 2] = tile.astype(BF16)

    transpose(0)
    pl.semaphore_wait(barrier, 31 + 7 + 2)

    mine16 = pl.ds(pl.multiple_of(16 * i, 16), 16)
    rows8 = pl.ds(pl.multiple_of(8 * i, 8), 8)
    large_copies = [
        remote(large_f.at[:, 1, rows8, :], large_f.at[:, 3, rows8, :], ls_sem.at[0], lr_sem.at[0], side_dev[0]),
        remote(large_f.at[:, 2, rows8, :], large_f.at[:, 0, rows8, :], ls_sem.at[1], lr_sem.at[1], side_dev[1]),
    ]
    for copy in large_copies:
        copy.start()

    def send_step(t, carry):
        @pl.when(t < 7)
        def _():
            transpose(t + 1)

        for d in range(1, 8):
            target = lax.rem(i + d, 8)
            remote(
                send.at[8 * target + t], cols.at[t + 1, :, :, mine16, :],
                xs_sem.at[t + 1], xr_sem.at[t + 1], {"slab": slab, "snap": target},
            ).start()
        pltpu.make_async_copy(
            send.at[8 * i + t], cols.at[t + 1, :, :, mine16, :], xr_sem.at[t + 1]
        ).start()
        return carry

    lax.fori_loop(0, 8, send_step, 0)
    for slot, shift in ((0, 63), (9, 8)):
        for d in range(1, 8):
            target = lax.rem(i + d, 8)
            remote(
                send.at[lax.rem(8 * target + shift, 64), pl.ds(1, 2)],
                cols.at[slot, pl.ds(1, 2), :, mine16, :],
                xs_sem.at[slot], xr_sem.at[slot], {"slab": slab, "snap": target},
            ).start()
        pltpu.make_async_copy(
            send.at[lax.rem(8 * i + shift, 64), pl.ds(1, 2)],
            cols.at[slot, pl.ds(1, 2), :, mine16, :], xr_sem.at[slot],
        ).start()

    mod_in.wait()

    def spread(k, carry):
        column = lax.rem(8 * i + k + 63, 64)
        mod_b[k] = jnp.broadcast_to(mod_v[pl.ds(column, 1), :], (128, 128)).T
        return carry

    lax.fori_loop(0, 10, spread, 0)
    met_in.wait()
    for copy in large_copies:
        copy.wait()

    @pl.when(slab == 0)
    def _():
        large_f[:, 0] = jnp.zeros((3, 64, 128), F32)

    @pl.when(slab == 31)
    def _():
        large_f[:, 3] = jnp.zeros((3, 64, 128), F32)

    acc[...] = jnp.zeros((128, 256), F32)

    def pass_on(xx):
        wait_bytes(cols.at[xx], xr_sem.at[xx])
        for side in range(2):
            remote(
                cols.at[xx, :, side], halo.at[1 - side, xx - 1],
                hs_sem.at[side, xx - 1], hr_sem.at[1 - side, xx - 1], side_dev[side],
            ).start()

    def pass_step(k, carry):
        pass_on(k + 1)
        return carry

    lax.fori_loop(0, 3, pass_step, 0)

    def column(k, carry):
        xx = lax.rem(k + 1, 8) + 1

        @pl.when(k < 5)
        def _():
            pass_on(k + 4)

        @pl.when(k == 6)
        def _():
            wait_bytes(cols.at[0, pl.ds(1, 2)], xr_sem.at[0])
            wait_bytes(cols.at[9, pl.ds(1, 2)], xr_sem.at[9])

        for side in range(2):
            wait_bytes(halo.at[side, xx - 1], hr_sem.at[side, xx - 1])

        @pl.when(slab == 0)
        def _():
            halo[0, xx - 1] = jnp.zeros((3, 128, 128), BF16)

        @pl.when(slab == 31)
        def _():
            halo[1, xx - 1] = jnp.zeros((3, 128, 128), BF16)

        here = 8 * i + xx - 1
        before = lax.rem(here + 63, 64)
        after = lax.rem(here + 1, 64)
        base = [[large_f[c, p, pl.ds(here, 1), :] for p in range(4)] for c in range(3)]
        base_m = [[large_f[c, p + 1, pl.ds(before, 1), :] for p in range(2)] for c in (1, 2)]
        base_p = [[large_f[c, p + 1, pl.ds(after, 1), :] for p in range(2)] for c in (1, 2)]
        half = [[0.5 * met[m, p, pl.ds(xx - 1, 1), :] for p in range(2)] for m in range(4)]
        lanes = pl.ds(pl.multiple_of(128 * (xx - 1), 128), 128)

        def snaps(s, inner):
            r = pl.ds(pl.multiple_of(16 * s, 16), 16)
            m0 = mod_b[xx, r, :]
            mm = mod_b[xx - 1, r, :]
            mp = mod_b[xx + 1, r, :]

            def field(c):
                return [
                    halo[0, xx - 1, c, r, :].astype(F32) + m0 * base[c][0],
                    cols[xx, c, 0, r, :].astype(F32) + m0 * base[c][1],
                    cols[xx, c, 1, r, :].astype(F32) + m0 * base[c][2],
                    halo[1, xx - 1, c, r, :].astype(F32) + m0 * base[c][3],
                ]

            def along_x(c, p):
                right = cols[xx + 1, c, p, r, :].astype(F32) + mp * base_p[c - 1][p]
                left = cols[xx - 1, c, p, r, :].astype(F32) + mm * base_m[c - 1][p]
                return right - left

            def along_z(f):
                return pltpu.roll(f, 127, 1) - pltpu.roll(f, 1, 1)

            u, v, w = field(0), field(1), field(2)
            for p in range(2):
                gx, sxy, gy, gz = (half[m][p] for m in range(4))
                du = u[p + 2] - u[p]
                dv = v[p + 2] - v[p]
                dw = w[p + 2] - w[p]
                around = (
                    gy * dw - gz * along_z(v[p + 1]),
                    gz * along_z(u[p + 1]) - (gx * along_x(2, p) + sxy * dw),
                    (gx * along_x(1, p) + sxy * dv) - gy * du,
                )
                for c in range(3):
                    high = around[c].astype(BF16)
                    vh[2 * c + p, r, lanes] = high
                    vl[2 * c + p, r, lanes] = (around[c] - high.astype(F32)).astype(BF16)
            return inner

        lax.fori_loop(0, 8, snaps, 0)
        rows_h = jnp.concatenate([vh[cy, :, lanes] for cy in range(6)], axis=1)
        rows_l = jnp.concatenate([vl[cy, :, lanes] for cy in range(6)], axis=1)
        both = jnp.concatenate([rows_h, rows_l], axis=0)
        acc[...] += lax.dot_general(
            rows_h, both, (((1,), (1,)), ((), ())), preferred_element_type=F32
        )
        return carry

    lax.fori_loop(0, 8, column, 0)
    half_gram = 0.5 * acc[:, :128] + acc[:, 128:]
    for k in range(32):
        gs[k] = half_gram[4 * k : 4 * k + 4, :]

    def exchange(stage, count, mine, device_of, src_of, dst):
        def one(d, carry):
            target = lax.rem(mine + d, count)
            remote(
                src_of(target), dst.at[mine], as_sem.at[stage], ar_sem.at[stage], device_of(target)
            ).start()
            return carry

        lax.fori_loop(1, count, one, 0)
        pltpu.make_async_copy(src_of(mine), dst.at[mine], ar_sem.at[stage]).start()
        wait_bytes(dst, ar_sem.at[stage])

    exchange(0, 32, q, plane_dev, lambda k: gs.at[k], rx)
    zs[...] = jnp.sum(rx[...], axis=0)
    exchange(1, 8, z, column_dev, lambda k: zs, rz)
    ag[...] = jnp.sum(rz[...], axis=0)
    exchange(2, 32, q, plane_dev, lambda k: ag, gf)
    g_out[...] = gf[...]

    for t in range(8):
        wait_bytes(send.at[pl.ds(0, 7)], xs_sem.at[t + 1])
    for slot in (0, 9):
        wait_bytes(send.at[pl.ds(0, 7), pl.ds(1, 2)], xs_sem.at[slot])
    for side in range(2):
        for k in range(8):
            wait_bytes(cols.at[k + 1, :, side], hs_sem.at[side, k])
    wait_bytes(rx.at[pl.ds(0, 31)], as_sem.at[0])
    wait_bytes(rz.at[pl.ds(0, 7)], as_sem.at[1])
    wait_bytes(gf.at[pl.ds(0, 31)], as_sem.at[2])


def gather(flow, large, mod_t, metric):
    vmem = pl.BlockSpec(memory_space=pltpu.VMEM)
    dma = pltpu.SemaphoreType.DMA
    return pl.pallas_call(
        gather_kernel,
        name="gather",
        out_shape=(
            pltpu.VMEM((6, 128, 1024), BF16),
            pltpu.VMEM((6, 128, 1024), BF16),
            pltpu.VMEM((32, 4, 128), F32),
        ),
        in_specs=[pl.BlockSpec(memory_space=pltpu.HBM)] * 4,
        out_specs=(vmem, vmem, vmem),
        scratch_shapes=[
            pltpu.VMEM((16, 384, 128), BF16),
            pltpu.VMEM((6144, 128), F32),
            pltpu.VMEM((64, 3, 2, 16, 128), BF16),
            pltpu.VMEM((10, 3, 2, 128, 128), BF16),
            pltpu.VMEM((2, 8, 3, 128, 128), BF16),
            pltpu.VMEM((3, 2, 64, 128), BF16),
            pltpu.VMEM((3, 4, 64, 128), F32),
            pltpu.VMEM((64, 128), F32),
            pltpu.VMEM((10, 128, 128), F32),
            pltpu.VMEM((4, 2, 8, 128), F32),
            pltpu.VMEM((128, 256), F32),
            pltpu.VMEM((32, 4, 128), F32),
            pltpu.VMEM((32, 4, 128), F32),
            pltpu.VMEM((4, 128), F32),
            pltpu.VMEM((8, 4, 128), F32),
            pltpu.VMEM((4, 128), F32),
            pltpu.VMEM((32, 4, 128), F32),
            dma((3,)), dma, dma((10,)), dma((10,)), dma((2, 8)), dma((2, 8)),
            dma((2,)), dma((2,)), dma((3,)), dma((3,)),
        ],
        compiler_params=pltpu.CompilerParams(
            collective_id=0, has_side_effects=True, vmem_limit_bytes=32 << 20
        ),
    )(flow, large, mod_t, metric)


def whiten_kernel(cells, vh, vl, g_ref, out_hbm, out_v, out_sem):
    half = g_ref[...].reshape(128, 128)
    correlation = (half + half.T) / cells
    eye = (
        lax.broadcasted_iota(jnp.int32, (128, 128), 0) == lax.broadcasted_iota(jnp.int32, (128, 128), 1)
    ).astype(F32)
    frob_scale = jnp.sqrt(jnp.sum(correlation * correlation, keepdims=True) + 1e-06)

    def halves(a):
        high = a.astype(BF16)
        return high, (a - high.astype(F32)).astype(BF16)

    def dot(a, b):
        a_high, a_low = halves(a)
        b_high, b_low = halves(b)
        left = jnp.concatenate([a_high, a_high, a_low], axis=1)
        right = jnp.concatenate([b_high, b_low, b_high], axis=0)
        return jnp.dot(left, right, preferred_element_type=F32)

    approx = correlation / frob_scale
    factor = 0.5 * (3.0 * eye - approx)
    approx = dot(approx, factor)
    inverse = factor
    for repeat in range(1, NSITER):
        factor = 0.5 * (3.0 * eye - dot(inverse, approx))
        if repeat < NSITER - 1:
            approx = dot(approx, factor)
        inverse = dot(factor, inverse)
    weights = inverse / jnp.sqrt(frob_scale)
    w_high = weights.astype(BF16)
    w_low = (weights - w_high.astype(F32)).astype(BF16)

    stores = []
    for k in range(6):
        high = vh[k]
        result = jnp.dot(w_high, high, preferred_element_type=F32)
        result += jnp.dot(w_high, vl[k], preferred_element_type=F32)
        result += jnp.dot(w_low, high, preferred_element_type=F32)
        for x in range(8):
            out_v[k, pl.ds(x, 128, stride=8), :] = result[:, 128 * x : 128 * (x + 1)]
        store = pltpu.make_async_copy(
            out_v.at[k].reshape(128, 8, 128), out_hbm.at[:, k // 2, k % 2], out_sem.at[k]
        )
        store.start()
        stores.append(store)
    for store in stores:
        store.wait()


def whiten(vh, vl, gram, cells):
    vmem = pl.BlockSpec(memory_space=pltpu.VMEM)
    return pl.pallas_call(
        functools.partial(whiten_kernel, cells),
        name="whiten",
        out_shape=jax.ShapeDtypeStruct((128, 3, 2, 8, 128), F32),
        in_specs=[vmem, vmem, vmem],
        out_specs=pl.BlockSpec(memory_space=pl.ANY),
        scratch_shapes=[pltpu.VMEM((6, 1024, 128), F32), pltpu.SemaphoreType.DMA((6,))],
        compiler_params=pltpu.CompilerParams(vmem_limit_bytes=32 << 20),
    )(vh, vl, gram)


def per_device(flow, large_scale, modulation, metric):
    sources = (flow.reshape(16, 384, 128), large_scale, modulation.T, metric)
    vh, vl, gram = gather(*(pltpu.with_memory_space_constraint(a, pltpu.HBM) for a in sources))
    return whiten(vh, vl, gram, 3.0 * 64 * 64 * 128)


def solution(mesh):
    return jax.shard_map(
        per_device,
        mesh=mesh,
        in_specs=(
            P("snap", None, "slab", None, None),
            P(None, "slab", None, None),
            P(),
            P(None, "slab", None, None),
        ),
        out_specs=P(None, None, "slab", "snap", None),
        check_vma=False,
    )
```

```python
import functools

import jax
import jax.numpy as jnp
from jax import lax
from jax.experimental import pallas as pl
from jax.experimental.pallas import tpu as pltpu
from jax.sharding import PartitionSpec as P

NSITER = 6
F32 = jnp.float32
BF16 = jnp.bfloat16
MESH = pl.DeviceIdType.MESH


def remote(src, dst, ssem, rsem, dev):
    return pltpu.make_async_remote_copy(
        src_ref=src, dst_ref=dst, send_sem=ssem, recv_sem=rsem, device_id=dev, device_id_type=MESH
    )


def wait_bytes(ref, sem):
    pltpu.make_async_copy(ref, ref, sem).wait()


def gather_kernel(
    flow_hbm, large_hbm, mod_hbm, metric_hbm,
    vh, vl, g_out,
    flow_v, flow_f, send, cols, halo, large_b, large_f, mod_v, mod_b, met,
    acc, gs, rx, zs, rz, ag, gf,
    in_sem, big_sem, xs_sem, xr_sem, hs_sem, hr_sem, ls_sem, lr_sem, as_sem, ar_sem, tokens,
):
    slab = lax.axis_index("slab")
    i = lax.axis_index("snap")
    z = slab // 4
    y = lax.rem(slab, 4)
    up = lax.rem(slab + 1, 32)
    down = lax.rem(slab + 31, 32)

    q = 8 * y + i
    side_dev = [{"slab": down, "snap": i}, {"slab": up, "snap": i}]
    z_side = [{"slab": lax.rem(slab + 4, 32), "snap": i}, {"slab": lax.rem(slab + 28, 32), "snap": i}]
    row_order = (4, 5, 2, 3, 6, 7, 1)
    row_dev = [{"slab": slab, "snap": i ^ d} for d in row_order]
    y_dev = [{"slab": slab ^ d, "snap": i} for d in (2, 1, 3)]
    barrier = pltpu.get_barrier_semaphore()
    greeted = row_dev + y_dev + side_dev + z_side
    for dev in greeted:
        pl.semaphore_signal(barrier, inc=1, device_id=dev, device_id_type=MESH)

    flow_in = [
        pltpu.make_async_copy(
            flow_hbm.at[pl.ds(4 * k, 4)], flow_v.at[pl.ds(4 * k, 4)], big_sem.at[k]
        )
        for k in range(4)
    ]
    for copy in flow_in:
        copy.start()
    large_in = pltpu.make_async_copy(large_hbm, large_b, in_sem.at[0])
    large_in.start()
    mod_in = pltpu.make_async_copy(mod_hbm, mod_v, in_sem.at[1])
    mod_in.start()
    met_in = pltpu.make_async_copy(
        metric_hbm.at[:, :, pl.ds(pl.multiple_of(8 * i, 8), 8), :], met, in_sem.at[2]
    )
    met_in.start()

    def widen(s, carry):
        for cy in range(6):
            for b in range(8):
                row = pl.multiple_of((cy * 8 + b) * 128 + 8 * s, 8)
                flow_f[pl.ds(row, 8), :] = flow_v[s, pl.ds(cy * 64 + 8 * b, 8), :].astype(F32)
        return carry

    for k in range(4):
        flow_in[k].wait()
        lax.fori_loop(4 * k, 4 * k + 4, widen, 0)

    def transpose(t):
        for b in range(8):
            for cy in range(6):
                tile = flow_f[pl.ds((cy * 8 + b) * 128 + t, 16, stride=8), :]
                send[8 * b + t, cy // 2, cy % 2] = tile.astype(BF16)

    transpose(0)
    pl.semaphore_wait(barrier, len(greeted))
    for dev in z_side:
        pl.semaphore_signal(tokens.at[0], inc=1, device_id=dev, device_id_type=MESH)

    mine16 = pl.ds(pl.multiple_of(16 * i, 16), 16)
    rows8 = pl.ds(pl.multiple_of(8 * i, 8), 8)
    def send_step(t, carry):
        @pl.when(t < 7)
        def _():
            transpose(t + 1)

        for d in row_order:
            target = i ^ d
            remote(
                send.at[8 * target + t], cols.at[t + 1, :, :, mine16, :],
                xs_sem.at[t + 1], xr_sem.at[t + 1], {"slab": slab, "snap": target},
            ).start()
        pltpu.make_async_copy(
            send.at[8 * i + t], cols.at[t + 1, :, :, mine16, :], xr_sem.at[t + 1]
        ).start()
        return carry

    lax.fori_loop(0, 8, send_step, 0)
    for slot, shift in ((0, 63), (9, 8)):
        for d in row_order:
            target = i ^ d
            remote(
                send.at[lax.rem(8 * target + shift, 64), pl.ds(1, 2)],
                cols.at[slot, pl.ds(1, 2), :, mine16, :],
                xs_sem.at[slot], xr_sem.at[slot], {"slab": slab, "snap": target},
            ).start()
        pltpu.make_async_copy(
            send.at[lax.rem(8 * i + shift, 64), pl.ds(1, 2)],
            cols.at[slot, pl.ds(1, 2), :, mine16, :], xr_sem.at[slot],
        ).start()

    large_in.wait()
    for c in range(3):
        for p in range(2):
            large_f[c, p + 1] = large_b[c, p].astype(F32)
    pl.semaphore_wait(tokens.at[0], 2)
    for dev in z_side:
        pl.semaphore_signal(tokens.at[1], inc=1, device_id=dev, device_id_type=MESH)
    mod_in.wait()

    def spread(k, carry):
        column = lax.rem(8 * i + k + 63, 64)
        mod_b[k] = jnp.broadcast_to(mod_v[pl.ds(column, 1), :], (128, 128)).T
        return carry

    lax.fori_loop(0, 10, spread, 0)
    large_copies = [
        remote(large_f.at[:, 1, rows8, :], large_f.at[:, 3, rows8, :], ls_sem.at[0], lr_sem.at[0], side_dev[0]),
        remote(large_f.at[:, 2, rows8, :], large_f.at[:, 0, rows8, :], ls_sem.at[1], lr_sem.at[1], side_dev[1]),
    ]
    for copy in large_copies:
        copy.start()

    pl.semaphore_wait(tokens.at[1], 2)
    for dev in z_side:
        pl.semaphore_signal(tokens.at[2], inc=1, device_id=dev, device_id_type=MESH)
    met_in.wait()
    acc[...] = jnp.zeros((128, 256), F32)

    def pass_on(xx):
        wait_bytes(cols.at[xx], xr_sem.at[xx])
        for side in range(2):
            remote(
                cols.at[xx, :, side], halo.at[1 - side, xx - 1],
                hs_sem.at[side, xx - 1], hr_sem.at[1 - side, xx - 1], side_dev[side],
            ).start()

    def pass_step(k, carry):
        pass_on(k + 1)
        return carry

    lax.fori_loop(0, 3, pass_step, 0)
    for copy in large_copies:
        copy.wait()

    @pl.when(slab == 0)
    def _():
        large_f[:, 0] = jnp.zeros((3, 64, 128), F32)

    @pl.when(slab == 31)
    def _():
        large_f[:, 3] = jnp.zeros((3, 64, 128), F32)


    def column(k, carry):
        xx = lax.rem(k + 1, 8) + 1

        @pl.when(k < 5)
        def _():
            pass_on(k + 4)

        @pl.when(k == 6)
        def _():
            wait_bytes(cols.at[0, pl.ds(1, 2)], xr_sem.at[0])
            wait_bytes(cols.at[9, pl.ds(1, 2)], xr_sem.at[9])

        for side in range(2):
            wait_bytes(halo.at[side, xx - 1], hr_sem.at[side, xx - 1])

        @pl.when(slab == 0)
        def _():
            halo[0, xx - 1] = jnp.zeros((3, 128, 128), BF16)

        @pl.when(slab == 31)
        def _():
            halo[1, xx - 1] = jnp.zeros((3, 128, 128), BF16)

        here = 8 * i + xx - 1
        before = lax.rem(here + 63, 64)
        after = lax.rem(here + 1, 64)
        base = [[large_f[c, p, pl.ds(here, 1), :] for p in range(4)] for c in range(3)]
        base_m = [[large_f[c, p + 1, pl.ds(before, 1), :] for p in range(2)] for c in (1, 2)]
        base_p = [[large_f[c, p + 1, pl.ds(after, 1), :] for p in range(2)] for c in (1, 2)]
        half = [[0.5 * met[m, p, pl.ds(xx - 1, 1), :] for p in range(2)] for m in range(4)]
        lanes = pl.ds(pl.multiple_of(128 * (xx - 1), 128), 128)

        def snaps(s, inner):
            r = pl.ds(pl.multiple_of(16 * s, 16), 16)
            m0 = mod_b[xx, r, :]
            mm = mod_b[xx - 1, r, :]
            mp = mod_b[xx + 1, r, :]

            def field(c):
                return [
                    halo[0, xx - 1, c, r, :].astype(F32) + m0 * base[c][0],
                    cols[xx, c, 0, r, :].astype(F32) + m0 * base[c][1],
                    cols[xx, c, 1, r, :].astype(F32) + m0 * base[c][2],
                    halo[1, xx - 1, c, r, :].astype(F32) + m0 * base[c][3],
                ]

            def along_x(c, p):
                right = cols[xx + 1, c, p, r, :].astype(F32) + mp * base_p[c - 1][p]
                left = cols[xx - 1, c, p, r, :].astype(F32) + mm * base_m[c - 1][p]
                return right - left

            def along_z(f):
                return pltpu.roll(f, 127, 1) - pltpu.roll(f, 1, 1)

            u, v, w = field(0), field(1), field(2)
            for p in range(2):
                gx, sxy, gy, gz = (half[m][p] for m in range(4))
                du = u[p + 2] - u[p]
                dv = v[p + 2] - v[p]
                dw = w[p + 2] - w[p]
                around = (
                    gy * dw - gz * along_z(v[p + 1]),
                    gz * along_z(u[p + 1]) - (gx * along_x(2, p) + sxy * dw),
                    (gx * along_x(1, p) + sxy * dv) - gy * du,
                )
                for c in range(3):
                    high = around[c].astype(BF16)
                    vh[2 * c + p, r, lanes] = high
                    vl[2 * c + p, r, lanes] = (around[c] - high.astype(F32)).astype(BF16)
            return inner

        lax.fori_loop(0, 8, snaps, 0, unroll=2)
        rows_h = jnp.concatenate([vh[cy, :, lanes] for cy in range(6)], axis=1)
        rows_l = jnp.concatenate([vl[cy, :, lanes] for cy in range(6)], axis=1)
        both = jnp.concatenate([rows_h, rows_l], axis=0)
        acc[...] += lax.dot_general(
            rows_h, both, (((1,), (1,)), ((), ())), preferred_element_type=F32
        )
        return carry

    lax.fori_loop(0, 8, column, 0)
    half_gram = 0.5 * acc[:, :128] + acc[:, 128:]
    for k in range(32):
        gs[k] = half_gram[4 * k : 4 * k + 4, :]

    plane_order = sorted(range(1, 32), key=lambda d: -(2 * ((d >> 4) & 1) + 2 * ((d >> 2) & 1) + ((d >> 3) & 1) + ((d >> 1) & 1)))
    plane = [(q ^ d, {"slab": slab ^ (d >> 3), "snap": i ^ (d & 7)}) for d in plane_order]
    line = [(z ^ d, {"slab": slab ^ (4 * d), "snap": i}) for d in (4, 5, 3, 7, 6, 2, 1)]

    def exchange(stage, mine, partners, src_of, dst):
        for target, dev in partners:
            remote(src_of(target), dst.at[mine], as_sem.at[stage], ar_sem.at[stage], dev).start()
        pltpu.make_async_copy(src_of(mine), dst.at[mine], ar_sem.at[stage]).start()
        wait_bytes(dst, ar_sem.at[stage])

    pl.semaphore_wait(tokens.at[2], 2)
    exchange(0, q, plane, lambda k: gs.at[k], rx)
    zs[...] = jnp.sum(rx[...], axis=0)
    exchange(1, z, line, lambda k: zs, rz)
    ag[...] = jnp.sum(rz[...], axis=0)
    exchange(2, q, plane, lambda k: ag, gf)
    g_out[...] = gf[...]

    for t in range(8):
        wait_bytes(send.at[pl.ds(0, 7)], xs_sem.at[t + 1])
    for slot in (0, 9):
        wait_bytes(send.at[pl.ds(0, 7), pl.ds(1, 2)], xs_sem.at[slot])
    for side in range(2):
        for k in range(8):
            wait_bytes(cols.at[k + 1, :, side], hs_sem.at[side, k])
    wait_bytes(rx.at[pl.ds(0, 31)], as_sem.at[0])
    wait_bytes(rz.at[pl.ds(0, 7)], as_sem.at[1])
    wait_bytes(gf.at[pl.ds(0, 31)], as_sem.at[2])


def gather(flow, large, mod_t, metric):
    vmem = pl.BlockSpec(memory_space=pltpu.VMEM)
    dma = pltpu.SemaphoreType.DMA
    return pl.pallas_call(
        gather_kernel,
        name="gather",
        out_shape=(
            pltpu.VMEM((6, 128, 1024), BF16),
            pltpu.VMEM((6, 128, 1024), BF16),
            pltpu.VMEM((32, 4, 128), F32),
        ),
        in_specs=[pl.BlockSpec(memory_space=pltpu.HBM)] * 4,
        out_specs=(vmem, vmem, vmem),
        scratch_shapes=[
            pltpu.VMEM((16, 384, 128), BF16),
            pltpu.VMEM((6144, 128), F32),
            pltpu.VMEM((64, 3, 2, 16, 128), BF16),
            pltpu.VMEM((10, 3, 2, 128, 128), BF16),
            pltpu.VMEM((2, 8, 3, 128, 128), BF16),
            pltpu.VMEM((3, 2, 64, 128), BF16),
            pltpu.VMEM((3, 4, 64, 128), F32),
            pltpu.VMEM((64, 128), F32),
            pltpu.VMEM((10, 128, 128), F32),
            pltpu.VMEM((4, 2, 8, 128), F32),
            pltpu.VMEM((128, 256), F32),
            pltpu.VMEM((32, 4, 128), F32),
            pltpu.VMEM((32, 4, 128), F32),
            pltpu.VMEM((4, 128), F32),
            pltpu.VMEM((8, 4, 128), F32),
            pltpu.VMEM((4, 128), F32),
            pltpu.VMEM((32, 4, 128), F32),
            dma((3,)), dma((4,)), dma((10,)), dma((10,)), dma((2, 8)), dma((2, 8)),
            dma((2,)), dma((2,)), dma((3,)), dma((3,)),
            pltpu.SemaphoreType.REGULAR((3,)),
        ],
        compiler_params=pltpu.CompilerParams(
            collective_id=0, has_side_effects=True, vmem_limit_bytes=32 << 20
        ),
    )(flow, large, mod_t, metric)


def whiten_kernel(cells, vh, vl, g_ref, out_hbm, out_v, out_sem):
    half = g_ref[...].reshape(128, 128)
    correlation = (half + half.T) / cells
    eye = (
        lax.broadcasted_iota(jnp.int32, (128, 128), 0) == lax.broadcasted_iota(jnp.int32, (128, 128), 1)
    ).astype(F32)
    frob_scale = jnp.sqrt(jnp.sum(correlation * correlation, keepdims=True) + 1e-06)

    def halves(a):
        high = a.astype(BF16)
        return high, (a - high.astype(F32)).astype(BF16)

    def dot(a, b):
        a_high, a_low = halves(a)
        b_high, b_low = halves(b)
        left = jnp.concatenate([a_high, a_high, a_low], axis=1)
        right = jnp.concatenate([b_high, b_low, b_high], axis=0)
        return jnp.dot(left, right, preferred_element_type=F32)

    approx = correlation / frob_scale
    factor = 0.5 * (3.0 * eye - approx)
    approx = dot(approx, factor)
    inverse = factor
    for repeat in range(1, NSITER):
        factor = 0.5 * (3.0 * eye - dot(inverse, approx))
        if repeat < NSITER - 1:
            approx = dot(approx, factor)
        inverse = dot(factor, inverse)
    weights = inverse / jnp.sqrt(frob_scale)
    w_high = weights.astype(BF16)
    w_low = (weights - w_high.astype(F32)).astype(BF16)

    stores = []
    for k in range(6):
        high = vh[k]
        result = jnp.dot(w_high, high, preferred_element_type=F32)
        result += jnp.dot(w_high, vl[k], preferred_element_type=F32)
        result += jnp.dot(w_low, high, preferred_element_type=F32)
        for x in range(8):
            out_v[k, pl.ds(x, 128, stride=8), :] = result[:, 128 * x : 128 * (x + 1)]
        store = pltpu.make_async_copy(
            out_v.at[k].reshape(128, 8, 128), out_hbm.at[:, k // 2, k % 2], out_sem.at[k]
        )
        store.start()
        stores.append(store)
    for store in stores:
        store.wait()


def whiten(vh, vl, gram, cells):
    vmem = pl.BlockSpec(memory_space=pltpu.VMEM)
    return pl.pallas_call(
        functools.partial(whiten_kernel, cells),
        name="whiten",
        out_shape=jax.ShapeDtypeStruct((128, 3, 2, 8, 128), F32),
        in_specs=[vmem, vmem, vmem],
        out_specs=pl.BlockSpec(memory_space=pl.ANY),
        scratch_shapes=[pltpu.VMEM((6, 1024, 128), F32), pltpu.SemaphoreType.DMA((6,))],
        compiler_params=pltpu.CompilerParams(vmem_limit_bytes=32 << 20),
    )(vh, vl, gram)


def per_device(flow, large_scale, modulation, metric):
    sources = (flow.reshape(16, 384, 128), large_scale, modulation.T, metric)
    vh, vl, gram = gather(*(pltpu.with_memory_space_constraint(a, pltpu.HBM) for a in sources))
    return whiten(vh, vl, gram, 3.0 * 64 * 64 * 128)


def solution(mesh):
    return jax.shard_map(
        per_device,
        mesh=mesh,
        in_specs=(
            P("snap", None, "slab", None, None),
            P(None, "slab", None, None),
            P(),
            P(None, "slab", None, None),
        ),
        out_specs=P(None, None, "slab", "snap", None),
        check_vma=False,
    )
```

```python
import functools

import jax
import jax.numpy as jnp
from jax import lax
from jax.experimental import pallas as pl
from jax.experimental.pallas import tpu as pltpu
from jax.sharding import PartitionSpec as P

NSITER = 6
F32 = jnp.float32
BF16 = jnp.bfloat16
MESH = pl.DeviceIdType.MESH


def remote(src, dst, ssem, rsem, dev):
    return pltpu.make_async_remote_copy(
        src_ref=src, dst_ref=dst, send_sem=ssem, recv_sem=rsem, device_id=dev, device_id_type=MESH
    )


def wait_bytes(ref, sem):
    pltpu.make_async_copy(ref, ref, sem).wait()


def gather_kernel(
    flow_hbm, large_hbm, mod_hbm, metric_hbm,
    vh, vl, g_out,
    flow_v, flow_f, send, cols, halo, large_b, large_f, mod_v, mod_b, met,
    acc, gs, rx, zs, rz, ag, gf,
    in_sem, big_sem, xs_sem, xr_sem, hs_sem, hr_sem, ls_sem, lr_sem, as_sem, ar_sem, edge_sem, tokens,
):
    slab = lax.axis_index("slab")
    i = lax.axis_index("snap")
    z = slab // 4
    y = lax.rem(slab, 4)
    up = lax.rem(slab + 1, 32)
    down = lax.rem(slab + 31, 32)

    q = 8 * y + i
    side_dev = [{"slab": down, "snap": i}, {"slab": up, "snap": i}]
    z_side = [{"slab": lax.rem(slab + 4, 32), "snap": i}, {"slab": lax.rem(slab + 28, 32), "snap": i}]
    row_order = (4, 5, 2, 3, 6, 7, 1)
    row_dev = [{"slab": slab, "snap": i ^ d} for d in row_order]
    y_dev = [{"slab": slab ^ d, "snap": i} for d in (2, 1, 3)]
    barrier = pltpu.get_barrier_semaphore()
    greeted = row_dev + y_dev + side_dev + z_side
    for dev in greeted:
        pl.semaphore_signal(barrier, inc=1, device_id=dev, device_id_type=MESH)

    flow_in = [
        pltpu.make_async_copy(
            flow_hbm.at[:, pl.ds(128 * c, 128)], flow_v.at[:, pl.ds(128 * c, 128)], big_sem.at[c]
        )
        for c in range(3)
    ]
    for copy in flow_in:
        copy.start()
    large_in = pltpu.make_async_copy(large_hbm, large_b, in_sem.at[0])
    large_in.start()
    mod_in = pltpu.make_async_copy(mod_hbm, mod_v, in_sem.at[1])
    mod_in.start()
    met_in = pltpu.make_async_copy(
        metric_hbm.at[:, :, pl.ds(pl.multiple_of(8 * i, 8), 8), :], met, in_sem.at[2]
    )
    met_in.start()

    def widen(c):
        def one(s, carry):
            for p in range(2):
                for b in range(8):
                    cy = 2 * c + p
                    row = pl.multiple_of((cy * 8 + b) * 128 + 8 * s, 8)
                    flow_f[pl.ds(row, 8), :] = flow_v[s, pl.ds(cy * 64 + 8 * b, 8), :].astype(F32)
            return carry

        lax.fori_loop(0, 16, one, 0)

    def transpose(t, c):
        for b in range(8):
            for p in range(2):
                tile = flow_f[pl.ds(((2 * c + p) * 8 + b) * 128 + t, 16, stride=8), :]
                send[8 * b + t, c, p] = tile.astype(BF16)

    def block(d):
        return pl.ds(16 * d, 16)

    rows8 = pl.ds(pl.multiple_of(8 * i, 8), 8)

    def send_unit(t, c):
        for side in range(2):
            remote(
                send.at[8 * i + t, c, side], halo.at[1 - side, t, c, block(0)],
                hs_sem.at[side, t], hr_sem.at[1 - side, t], side_dev[side],
            ).start()
        for d in row_order:
            target = i ^ d
            remote(
                send.at[8 * target + t, c], cols.at[t + 1, c, :, block(d), :],
                xs_sem.at[t + 1], xr_sem.at[t + 1, c], {"slab": slab, "snap": target},
            ).start()
        pltpu.make_async_copy(
            send.at[8 * i + t, c], cols.at[t + 1, c, :, block(0), :], xr_sem.at[t + 1, c]
        ).start()

    flow_in[0].wait()
    widen(0)
    transpose(0, 0)
    pl.semaphore_wait(barrier, len(greeted))
    for c in (1, 2):
        flow_in[c].wait()
        send_unit(0, c - 1)
        if c == 1:
            for dev in z_side:
                pl.semaphore_signal(tokens.at[0], inc=1, device_id=dev, device_id_type=MESH)
        widen(c)
        transpose(0, c)

    def send_step(u, carry):
        @pl.when(u < 23)
        def _():
            transpose(lax.div(u + 1, 3), lax.rem(u + 1, 3))

        send_unit(lax.div(u, 3), lax.rem(u, 3))
        return carry

    lax.fori_loop(2, 24, send_step, 0)

    def edge_of(k):
        core = lax.rem(k, 2)
        return send.at[lax.rem(8 * k + 63 + 9 * core, 64), pl.ds(1, 2)], 9 * core

    for d in row_order:
        target = i ^ d
        source, slot = edge_of(target)
        remote(
            source, cols.at[slot, pl.ds(1, 2), :, block(d), :],
            edge_sem.at[0], xr_sem.at[slot, 0], {"slab": slab, "snap": target},
        ).start()
    source, slot = edge_of(i)
    pltpu.make_async_copy(
        source, cols.at[slot, pl.ds(1, 2), :, block(0), :], xr_sem.at[slot, 0]
    ).start()
    large_in.wait()
    for c in range(3):
        for p in range(2):
            large_f[c, p + 1] = large_b[c, p].astype(F32)
    pl.semaphore_wait(tokens.at[0], 2)
    for dev in z_side:
        pl.semaphore_signal(tokens.at[1], inc=1, device_id=dev, device_id_type=MESH)
    mod_in.wait()

    def spread(k, carry):
        column = lax.rem(8 * i + k + 63, 64)
        mod_b[k] = jnp.broadcast_to(mod_v[pl.ds(column, 1), :], (128, 128)).T
        return carry

    lax.fori_loop(0, 10, spread, 0)
    large_copies = [
        remote(large_f.at[:, 1, rows8, :], large_f.at[:, 3, rows8, :], ls_sem.at[0], lr_sem.at[0], side_dev[0]),
        remote(large_f.at[:, 2, rows8, :], large_f.at[:, 0, rows8, :], ls_sem.at[1], lr_sem.at[1], side_dev[1]),
    ]
    for copy in large_copies:
        copy.start()

    pl.semaphore_wait(tokens.at[1], 2)
    for dev in z_side:
        pl.semaphore_signal(tokens.at[2], inc=1, device_id=dev, device_id_type=MESH)
    met_in.wait()
    acc[...] = jnp.zeros((128, 256), F32)

    rest = pl.ds(16, 112)

    def pass_on(xx, c):
        wait_bytes(cols.at[xx, c], xr_sem.at[xx, c])
        for side in range(2):
            remote(
                cols.at[xx, c, side, rest], halo.at[1 - side, xx - 1, c, rest],
                hs_sem.at[side, xx - 1], hr_sem.at[1 - side, xx - 1], side_dev[side],
            ).start()

    def pass_step(k, carry):
        for c in range(3):
            pass_on(k + 1, c)
        return carry

    lax.fori_loop(0, 4, pass_step, 0)
    for copy in large_copies:
        copy.wait()

    @pl.when(slab == 0)
    def _():
        large_f[:, 0] = jnp.zeros((3, 64, 128), F32)

    @pl.when(slab == 31)
    def _():
        large_f[:, 3] = jnp.zeros((3, 64, 128), F32)


    def column(k, carry):
        xx = k + 2 - 7 * lax.div(k, 6) + 6 * lax.div(k, 7)

        @pl.when(k < 4)
        def _():
            for c in range(3):
                pass_on(k + 5, c)

        @pl.when(k == 6)
        def _():
            wait_bytes(cols.at[0, pl.ds(1, 2)], xr_sem.at[0, 0])

        @pl.when(k == 7)
        def _():
            wait_bytes(cols.at[9, pl.ds(1, 2)], xr_sem.at[9, 0])

        for side in range(2):
            wait_bytes(halo.at[side, xx - 1], hr_sem.at[side, xx - 1])

        @pl.when(slab == 0)
        def _():
            halo[0, xx - 1] = jnp.zeros((3, 128, 128), BF16)

        @pl.when(slab == 31)
        def _():
            halo[1, xx - 1] = jnp.zeros((3, 128, 128), BF16)

        here = 8 * i + xx - 1
        before = lax.rem(here + 63, 64)
        after = lax.rem(here + 1, 64)
        base = [[large_f[c, p, pl.ds(here, 1), :] for p in range(4)] for c in range(3)]
        base_m = [[large_f[c, p + 1, pl.ds(before, 1), :] for p in range(2)] for c in (1, 2)]
        base_p = [[large_f[c, p + 1, pl.ds(after, 1), :] for p in range(2)] for c in (1, 2)]
        half = [[0.5 * met[m, p, pl.ds(xx - 1, 1), :] for p in range(2)] for m in range(4)]
        lanes = pl.ds(pl.multiple_of(128 * (xx - 1), 128), 128)

        def snaps(s, inner):
            r = pl.ds(pl.multiple_of(16 * s, 16), 16)
            own = pl.ds(pl.multiple_of(16 * (s ^ i), 16), 16)
            m0 = mod_b[xx, own, :]
            mm = mod_b[xx - 1, own, :]
            mp = mod_b[xx + 1, own, :]

            def field(c):
                return [
                    halo[0, xx - 1, c, r, :].astype(F32) + m0 * base[c][0],
                    cols[xx, c, 0, r, :].astype(F32) + m0 * base[c][1],
                    cols[xx, c, 1, r, :].astype(F32) + m0 * base[c][2],
                    halo[1, xx - 1, c, r, :].astype(F32) + m0 * base[c][3],
                ]

            def along_x(c, p):
                right = cols[xx + 1, c, p, r, :].astype(F32) + mp * base_p[c - 1][p]
                left = cols[xx - 1, c, p, r, :].astype(F32) + mm * base_m[c - 1][p]
                return right - left

            def along_z(f):
                return pltpu.roll(f, 127, 1) - pltpu.roll(f, 1, 1)

            u, v, w = field(0), field(1), field(2)
            for p in range(2):
                gx, sxy, gy, gz = (half[m][p] for m in range(4))
                du = u[p + 2] - u[p]
                dv = v[p + 2] - v[p]
                dw = w[p + 2] - w[p]
                around = (
                    gy * dw - gz * along_z(v[p + 1]),
                    gz * along_z(u[p + 1]) - (gx * along_x(2, p) + sxy * dw),
                    (gx * along_x(1, p) + sxy * dv) - gy * du,
                )
                for c in range(3):
                    high = around[c].astype(BF16)
                    vh[2 * c + p, own, lanes] = high
                    vl[2 * c + p, own, lanes] = (around[c] - high.astype(F32)).astype(BF16)
            return inner

        lax.fori_loop(0, 8, snaps, 0, unroll=4)

        @pl.when(k == 3)
        def _():
            core = lax.rem(i, 2)
            for b in range(8):
                remote(
                    cols.at[8 - 7 * core, pl.ds(1, 2), :, block(b), :],
                    cols.at[9 * core, pl.ds(1, 2), :, block(b ^ 1), :],
                    edge_sem.at[1], xr_sem.at[9 * core, 0], {"slab": slab, "snap": i ^ 1},
                ).start()

        rows_h = jnp.concatenate([vh[cy, :, lanes] for cy in range(6)], axis=1)
        rows_l = jnp.concatenate([vl[cy, :, lanes] for cy in range(6)], axis=1)
        both = jnp.concatenate([rows_h, rows_l], axis=0)
        acc[...] += lax.dot_general(
            rows_h, both, (((1,), (1,)), ((), ())), preferred_element_type=F32
        )
        return carry

    lax.fori_loop(0, 8, column, 0)
    half_gram = 0.5 * acc[:, :128] + acc[:, 128:]
    for k in range(32):
        gs[k] = half_gram[4 * k : 4 * k + 4, :]

    plane_order = sorted(range(1, 32), key=lambda d: -(2 * ((d >> 4) & 1) + 2 * ((d >> 2) & 1) + ((d >> 3) & 1) + ((d >> 1) & 1)))
    plane = [(q ^ d, {"slab": slab ^ (d >> 3), "snap": i ^ (d & 7)}) for d in plane_order]
    line = [(z ^ d, {"slab": slab ^ (4 * d), "snap": i}) for d in (4, 5, 3, 7, 6, 2, 1)]

    def exchange(stage, mine, partners, src_of, dst):
        for target, dev in partners:
            remote(src_of(target), dst.at[mine], as_sem.at[stage], ar_sem.at[stage], dev).start()
        pltpu.make_async_copy(src_of(mine), dst.at[mine], ar_sem.at[stage]).start()
        wait_bytes(dst, ar_sem.at[stage])

    pl.semaphore_wait(tokens.at[2], 2)
    exchange(0, q, plane, lambda k: gs.at[k], rx)
    zs[...] = jnp.sum(rx[...], axis=0)
    exchange(1, z, line, lambda k: zs, rz)
    ag[...] = jnp.sum(rz[...], axis=0)
    exchange(2, q, plane, lambda k: ag, gf)
    g_out[...] = gf[...]

    for t in range(8):
        wait_bytes(send.at[pl.ds(0, 7)], xs_sem.at[t + 1])
    wait_bytes(send.at[pl.ds(0, 7), pl.ds(1, 2)], edge_sem.at[0])
    wait_bytes(cols.at[0, pl.ds(1, 2)], edge_sem.at[1])
    for side in range(2):
        for k in range(8):
            wait_bytes(cols.at[k + 1, :, side], hs_sem.at[side, k])
    wait_bytes(rx.at[pl.ds(0, 31)], as_sem.at[0])
    wait_bytes(rz.at[pl.ds(0, 7)], as_sem.at[1])
    wait_bytes(gf.at[pl.ds(0, 31)], as_sem.at[2])


def gather(flow, large, mod_t, metric):
    vmem = pl.BlockSpec(memory_space=pltpu.VMEM)
    dma = pltpu.SemaphoreType.DMA
    return pl.pallas_call(
        gather_kernel,
        name="gather",
        out_shape=(
            pltpu.VMEM((6, 128, 1024), BF16),
            pltpu.VMEM((6, 128, 1024), BF16),
            pltpu.VMEM((32, 4, 128), F32),
        ),
        in_specs=[pl.BlockSpec(memory_space=pltpu.HBM)] * 4,
        out_specs=(vmem, vmem, vmem),
        scratch_shapes=[
            pltpu.VMEM((16, 384, 128), BF16),
            pltpu.VMEM((6144, 128), F32),
            pltpu.VMEM((64, 3, 2, 16, 128), BF16),
            pltpu.VMEM((10, 3, 2, 128, 128), BF16),
            pltpu.VMEM((2, 8, 3, 128, 128), BF16),
            pltpu.VMEM((3, 2, 64, 128), BF16),
            pltpu.VMEM((3, 4, 64, 128), F32),
            pltpu.VMEM((64, 128), F32),
            pltpu.VMEM((10, 128, 128), F32),
            pltpu.VMEM((4, 2, 8, 128), F32),
            pltpu.VMEM((128, 256), F32),
            pltpu.VMEM((32, 4, 128), F32),
            pltpu.VMEM((32, 4, 128), F32),
            pltpu.VMEM((4, 128), F32),
            pltpu.VMEM((8, 4, 128), F32),
            pltpu.VMEM((4, 128), F32),
            pltpu.VMEM((32, 4, 128), F32),
            dma((3,)), dma((3,)), dma((10,)), dma((10, 3)), dma((2, 8)), dma((2, 8)),
            dma((2,)), dma((2,)), dma((3,)), dma((3,)), dma((2,)),
            pltpu.SemaphoreType.REGULAR((3,)),
        ],
        compiler_params=pltpu.CompilerParams(
            collective_id=0, has_side_effects=True, vmem_limit_bytes=32 << 20
        ),
    )(flow, large, mod_t, metric)


def whiten_kernel(cells, vh, vl, g_ref, out_hbm, out_v, out_sem):
    half = g_ref[...].reshape(128, 128)
    correlation = (half + half.T) / cells
    eye = (
        lax.broadcasted_iota(jnp.int32, (128, 128), 0) == lax.broadcasted_iota(jnp.int32, (128, 128), 1)
    ).astype(F32)
    frob_scale = jnp.sqrt(jnp.sum(correlation * correlation, keepdims=True) + 1e-06)

    def halves(a):
        high = a.astype(BF16)
        return high, (a - high.astype(F32)).astype(BF16)

    def dot(a, b):
        a_high, a_low = halves(a)
        b_high, b_low = halves(b)
        left = jnp.concatenate([a_high, a_high, a_low], axis=1)
        right = jnp.concatenate([b_high, b_low, b_high], axis=0)
        return jnp.dot(left, right, preferred_element_type=F32)

    approx = correlation / frob_scale
    factor = 0.5 * (3.0 * eye - approx)
    approx = dot(approx, factor)
    inverse = factor
    for repeat in range(1, NSITER):
        factor = 0.5 * (3.0 * eye - dot(inverse, approx))
        if repeat < NSITER - 1:
            approx = dot(approx, factor)
        inverse = dot(factor, inverse)
    left = jnp.concatenate(
        [jnp.concatenate([w, w], axis=1) for w in halves(inverse / jnp.sqrt(frob_scale))], axis=0
    )

    stores = []
    for k in range(6):
        right = jnp.concatenate([vh[k], vl[k]], axis=0)
        parts = jnp.dot(left, right, preferred_element_type=F32)
        result = parts[:128] + parts[128:]
        for x in range(8):
            out_v[k, pl.ds(x, 128, stride=8), :] = result[:, 128 * x : 128 * (x + 1)]
        store = pltpu.make_async_copy(
            out_v.at[k].reshape(128, 8, 128), out_hbm.at[:, k // 2, k % 2], out_sem.at[k]
        )
        store.start()
        stores.append(store)
    for store in stores:
        store.wait()


def whiten(vh, vl, gram, cells):
    vmem = pl.BlockSpec(memory_space=pltpu.VMEM)
    return pl.pallas_call(
        functools.partial(whiten_kernel, cells),
        name="whiten",
        out_shape=jax.ShapeDtypeStruct((128, 3, 2, 8, 128), F32),
        in_specs=[vmem, vmem, vmem],
        out_specs=pl.BlockSpec(memory_space=pl.ANY),
        scratch_shapes=[pltpu.VMEM((6, 1024, 128), F32), pltpu.SemaphoreType.DMA((6,))],
        compiler_params=pltpu.CompilerParams(vmem_limit_bytes=32 << 20),
    )(vh, vl, gram)


def per_device(flow, large_scale, modulation, metric):
    sources = (flow.reshape(16, 384, 128), large_scale, modulation.T, metric)
    vh, vl, gram = gather(*(pltpu.with_memory_space_constraint(a, pltpu.HBM) for a in sources))
    return whiten(vh, vl, gram, 3.0 * 64 * 64 * 128)


def solution(mesh):
    return jax.shard_map(
        per_device,
        mesh=mesh,
        in_specs=(
            P("snap", None, "slab", None, None),
            P(None, "slab", None, None),
            P(),
            P(None, "slab", None, None),
        ),
        out_specs=P(None, None, "slab", "snap", None),
        check_vma=False,
    )
```

```python
import functools

import jax
import jax.numpy as jnp
from jax import lax
from jax.experimental import pallas as pl
from jax.experimental.pallas import tpu as pltpu
from jax.sharding import PartitionSpec as P

NSITER = 6
F32 = jnp.float32
BF16 = jnp.bfloat16
MESH = pl.DeviceIdType.MESH


def remote(src, dst, ssem, rsem, dev):
    return pltpu.make_async_remote_copy(
        src_ref=src, dst_ref=dst, send_sem=ssem, recv_sem=rsem, device_id=dev, device_id_type=MESH
    )


def wait_bytes(ref, sem):
    pltpu.make_async_copy(ref, ref, sem).wait()


def gather_kernel(
    flow_hbm, large_hbm, mod_hbm, metric_hbm,
    vh, vl, g_out,
    flow_v, flow_f, send, cols, halo, large_b, large_f, mod_v, mod_b, met,
    acc, gs, rx, zs, rz, ag, gf,
    in_sem, big_sem, xs_sem, xr_sem, hs_sem, hr_sem, ls_sem, lr_sem, as_sem, ar_sem, edge_sem, tokens,
):
    slab = lax.axis_index("slab")
    i = lax.axis_index("snap")
    z = slab // 4
    y = lax.rem(slab, 4)
    up = lax.rem(slab + 1, 32)
    down = lax.rem(slab + 31, 32)

    q = 8 * y + i
    side_dev = [{"slab": down, "snap": i}, {"slab": up, "snap": i}]
    z_side = [{"slab": lax.rem(slab + 4, 32), "snap": i}, {"slab": lax.rem(slab + 28, 32), "snap": i}]
    row_order = (4, 5, 2, 3, 6, 7, 1)
    row_dev = [{"slab": slab, "snap": i ^ d} for d in row_order]
    y_dev = [{"slab": slab ^ d, "snap": i} for d in (2, 1, 3)]
    barrier = pltpu.get_barrier_semaphore()
    cross_dev = [{"slab": down, "snap": i ^ 1}, {"slab": up, "snap": i ^ 1}]
    greeted = row_dev + y_dev + side_dev + cross_dev + z_side
    for dev in greeted:
        pl.semaphore_signal(barrier, inc=1, device_id=dev, device_id_type=MESH)

    flow_in = [
        pltpu.make_async_copy(
            flow_hbm.at[:, pl.ds(128 * c, 128)], flow_v.at[:, pl.ds(128 * c, 128)], big_sem.at[c]
        )
        for c in range(3)
    ]
    for copy in flow_in:
        copy.start()
    large_in = pltpu.make_async_copy(large_hbm, large_b, in_sem.at[0])
    large_in.start()
    mod_in = pltpu.make_async_copy(mod_hbm, mod_v, in_sem.at[1])
    mod_in.start()
    met_in = pltpu.make_async_copy(
        metric_hbm.at[:, :, pl.ds(pl.multiple_of(8 * i, 8), 8), :], met, in_sem.at[2]
    )
    met_in.start()

    def widen(c):
        def one(s, carry):
            for p in range(2):
                for b in range(8):
                    cy = 2 * c + p
                    row = pl.multiple_of((cy * 8 + b) * 128 + 8 * s, 8)
                    flow_f[pl.ds(row, 8), :] = flow_v[s, pl.ds(cy * 64 + 8 * b, 8), :].astype(F32)
            return carry

        lax.fori_loop(0, 16, one, 0)

    def transpose(t, c):
        for b in range(8):
            for p in range(2):
                tile = flow_f[pl.ds(((2 * c + p) * 8 + b) * 128 + t, 16, stride=8), :]
                send[8 * b + t, c, p] = tile.astype(BF16)

    def block(d):
        return pl.ds(16 * d, 16)

    rows8 = pl.ds(pl.multiple_of(8 * i, 8), 8)

    def send_unit(t, c):
        for e in range(2):
            for side in range(2):
                remote(
                    send.at[8 * (i ^ e) + t, c, side], halo.at[1 - side, t, c, block(e)],
                    hs_sem.at[side, t], hr_sem.at[1 - side, t],
                    {"slab": (down, up)[side], "snap": i ^ e},
                ).start()
        for d in row_order:
            target = i ^ d
            remote(
                send.at[8 * target + t, c], cols.at[t + 1, c, :, block(d), :],
                xs_sem.at[t + 1], xr_sem.at[t + 1, c], {"slab": slab, "snap": target},
            ).start()
        pltpu.make_async_copy(
            send.at[8 * i + t, c], cols.at[t + 1, c, :, block(0), :], xr_sem.at[t + 1, c]
        ).start()

    flow_in[0].wait()
    widen(0)
    transpose(0, 0)
    pl.semaphore_wait(barrier, len(greeted))
    for c in (1, 2):
        flow_in[c].wait()
        send_unit(0, c - 1)
        if c == 1:
            for dev in z_side:
                pl.semaphore_signal(tokens.at[0], inc=1, device_id=dev, device_id_type=MESH)
        widen(c)
        transpose(0, c)

    def send_step(u, carry):
        @pl.when(u < 23)
        def _():
            transpose(lax.div(u + 1, 3), lax.rem(u + 1, 3))

        send_unit(lax.div(u, 3), lax.rem(u, 3))
        return carry

    lax.fori_loop(2, 24, send_step, 0)

    def edge_of(k):
        core = lax.rem(k, 2)
        return send.at[lax.rem(8 * k + 63 + 9 * core, 64), pl.ds(1, 2)], 9 * core

    for d in row_order:
        target = i ^ d
        source, slot = edge_of(target)
        remote(
            source, cols.at[slot, pl.ds(1, 2), :, block(d), :],
            edge_sem.at[0], xr_sem.at[slot, 0], {"slab": slab, "snap": target},
        ).start()
    source, slot = edge_of(i)
    pltpu.make_async_copy(
        source, cols.at[slot, pl.ds(1, 2), :, block(0), :], xr_sem.at[slot, 0]
    ).start()
    large_in.wait()
    for c in range(3):
        for p in range(2):
            large_f[c, p + 1] = large_b[c, p].astype(F32)
    pl.semaphore_wait(tokens.at[0], 2)
    for dev in z_side:
        pl.semaphore_signal(tokens.at[1], inc=1, device_id=dev, device_id_type=MESH)
    mod_in.wait()

    def spread(k, carry):
        column = lax.rem(8 * i + k + 63, 64)
        mod_b[k] = jnp.broadcast_to(mod_v[pl.ds(column, 1), :], (128, 128)).T
        return carry

    lax.fori_loop(0, 10, spread, 0)
    large_copies = [
        remote(large_f.at[:, 1, rows8, :], large_f.at[:, 3, rows8, :], ls_sem.at[0], lr_sem.at[0], side_dev[0]),
        remote(large_f.at[:, 2, rows8, :], large_f.at[:, 0, rows8, :], ls_sem.at[1], lr_sem.at[1], side_dev[1]),
    ]
    for copy in large_copies:
        copy.start()

    pl.semaphore_wait(tokens.at[1], 2)
    for dev in z_side:
        pl.semaphore_signal(tokens.at[2], inc=1, device_id=dev, device_id_type=MESH)
    met_in.wait()
    acc[...] = jnp.zeros((128, 256), F32)

    rest = pl.ds(32, 96)

    def pass_on(xx, c):
        wait_bytes(cols.at[xx, c], xr_sem.at[xx, c])
        for side in range(2):
            remote(
                cols.at[xx, c, side, rest], halo.at[1 - side, xx - 1, c, rest],
                hs_sem.at[side, xx - 1], hr_sem.at[1 - side, xx - 1], side_dev[side],
            ).start()

    def pass_step(k, carry):
        for c in range(3):
            pass_on(k + 1, c)
        return carry

    lax.fori_loop(0, 3, pass_step, 0)
    for copy in large_copies:
        copy.wait()

    @pl.when(slab == 0)
    def _():
        large_f[:, 0] = jnp.zeros((3, 64, 128), F32)

    @pl.when(slab == 31)
    def _():
        large_f[:, 3] = jnp.zeros((3, 64, 128), F32)


    def column(k, carry):
        xx = k + 2 - 7 * lax.div(k, 6) + 6 * lax.div(k, 7)

        @pl.when(k < 5)
        def _():
            for c in range(3):
                pass_on(k + 4, c)

        @pl.when(k == 6)
        def _():
            wait_bytes(cols.at[0, pl.ds(1, 2)], xr_sem.at[0, 0])

        @pl.when(k == 7)
        def _():
            wait_bytes(cols.at[9, pl.ds(1, 2)], xr_sem.at[9, 0])

        for side in range(2):
            wait_bytes(halo.at[side, xx - 1], hr_sem.at[side, xx - 1])

        @pl.when(slab == 0)
        def _():
            halo[0, xx - 1] = jnp.zeros((3, 128, 128), BF16)

        @pl.when(slab == 31)
        def _():
            halo[1, xx - 1] = jnp.zeros((3, 128, 128), BF16)

        here = 8 * i + xx - 1
        before = lax.rem(here + 63, 64)
        after = lax.rem(here + 1, 64)
        base = [[large_f[c, p, pl.ds(here, 1), :] for p in range(4)] for c in range(3)]
        base_m = [[large_f[c, p + 1, pl.ds(before, 1), :] for p in range(2)] for c in (1, 2)]
        base_p = [[large_f[c, p + 1, pl.ds(after, 1), :] for p in range(2)] for c in (1, 2)]
        half = [[0.5 * met[m, p, pl.ds(xx - 1, 1), :] for p in range(2)] for m in range(4)]
        lanes = pl.ds(pl.multiple_of(128 * (xx - 1), 128), 128)

        def snaps(s, inner):
            r = pl.ds(pl.multiple_of(16 * s, 16), 16)
            own = pl.ds(pl.multiple_of(16 * (s ^ i), 16), 16)
            m0 = mod_b[xx, own, :]
            mm = mod_b[xx - 1, own, :]
            mp = mod_b[xx + 1, own, :]

            def field(c):
                return [
                    halo[0, xx - 1, c, r, :].astype(F32) + m0 * base[c][0],
                    cols[xx, c, 0, r, :].astype(F32) + m0 * base[c][1],
                    cols[xx, c, 1, r, :].astype(F32) + m0 * base[c][2],
                    halo[1, xx - 1, c, r, :].astype(F32) + m0 * base[c][3],
                ]

            def along_x(c, p):
                right = cols[xx + 1, c, p, r, :].astype(F32) + mp * base_p[c - 1][p]
                left = cols[xx - 1, c, p, r, :].astype(F32) + mm * base_m[c - 1][p]
                return right - left

            def along_z(f):
                return pltpu.roll(f, 127, 1) - pltpu.roll(f, 1, 1)

            u, v, w = field(0), field(1), field(2)
            for p in range(2):
                gx, sxy, gy, gz = (half[m][p] for m in range(4))
                du = u[p + 2] - u[p]
                dv = v[p + 2] - v[p]
                dw = w[p + 2] - w[p]
                around = (
                    gy * dw - gz * along_z(v[p + 1]),
                    gz * along_z(u[p + 1]) - (gx * along_x(2, p) + sxy * dw),
                    (gx * along_x(1, p) + sxy * dv) - gy * du,
                )
                for c in range(3):
                    high = around[c].astype(BF16)
                    vh[2 * c + p, own, lanes] = high
                    vl[2 * c + p, own, lanes] = (around[c] - high.astype(F32)).astype(BF16)
            return inner

        lax.fori_loop(0, 8, snaps, 0, unroll=4)

        @pl.when(k == 4)
        def _():
            core = lax.rem(i, 2)
            for b in range(8):
                remote(
                    cols.at[8 - 7 * core, pl.ds(1, 2), :, block(b), :],
                    cols.at[9 * core, pl.ds(1, 2), :, block(b ^ 1), :],
                    edge_sem.at[1], xr_sem.at[9 * core, 0], {"slab": slab, "snap": i ^ 1},
                ).start()

        rows_h = jnp.concatenate([vh[cy, :, lanes] for cy in range(6)], axis=1)
        rows_l = jnp.concatenate([vl[cy, :, lanes] for cy in range(6)], axis=1)
        both = jnp.concatenate([rows_h, rows_l], axis=0)
        acc[...] += lax.dot_general(
            rows_h, both, (((1,), (1,)), ((), ())), preferred_element_type=F32
        )
        return carry

    lax.fori_loop(0, 8, column, 0)
    half_gram = 0.5 * acc[:, :128] + acc[:, 128:]
    for k in range(32):
        gs[k] = half_gram[4 * k : 4 * k + 4, :]

    plane_order = sorted(range(1, 32), key=lambda d: -(2 * ((d >> 4) & 1) + 2 * ((d >> 2) & 1) + ((d >> 3) & 1) + ((d >> 1) & 1)))
    plane = [(q ^ d, {"slab": slab ^ (d >> 3), "snap": i ^ (d & 7)}) for d in plane_order]
    line = [(z ^ d, {"slab": slab ^ (4 * d), "snap": i}) for d in (4, 5, 3, 7, 6, 2, 1)]

    def exchange(stage, mine, partners, src_of, dst, drain):
        for target, dev in partners:
            remote(src_of(target), dst.at[mine], as_sem.at[stage], ar_sem.at[stage], dev).start()
        pltpu.make_async_copy(src_of(mine), dst.at[mine], ar_sem.at[stage]).start()
        drain()
        wait_bytes(dst, ar_sem.at[stage])

    def drain_columns():
        for t in range(8):
            wait_bytes(send.at[pl.ds(0, 7)], xs_sem.at[t + 1])
        wait_bytes(send.at[pl.ds(0, 7), pl.ds(1, 2)], edge_sem.at[0])
        wait_bytes(cols.at[0, pl.ds(1, 2)], edge_sem.at[1])
        for side in range(2):
            for k in range(8):
                wait_bytes(cols.at[k + 1, :, side], hs_sem.at[side, k])

    pl.semaphore_wait(tokens.at[2], 2)
    exchange(0, q, plane, lambda k: gs.at[k], rx, drain_columns)
    zs[...] = jnp.sum(rx[...], axis=0)
    exchange(1, z, line, lambda k: zs, rz, lambda: wait_bytes(rx.at[pl.ds(0, 31)], as_sem.at[0]))
    ag[...] = jnp.sum(rz[...], axis=0)
    exchange(2, q, plane, lambda k: ag, g_out, lambda: wait_bytes(rz.at[pl.ds(0, 7)], as_sem.at[1]))
    wait_bytes(g_out.at[pl.ds(0, 31)], as_sem.at[2])


def gather(flow, large, mod_t, metric):
    vmem = pl.BlockSpec(memory_space=pltpu.VMEM)
    dma = pltpu.SemaphoreType.DMA
    return pl.pallas_call(
        gather_kernel,
        name="gather",
        out_shape=(
            pltpu.VMEM((6, 128, 1024), BF16),
            pltpu.VMEM((6, 128, 1024), BF16),
            pltpu.VMEM((32, 4, 128), F32),
        ),
        in_specs=[pl.BlockSpec(memory_space=pltpu.HBM)] * 4,
        out_specs=(vmem, vmem, vmem),
        scratch_shapes=[
            pltpu.VMEM((16, 384, 128), BF16),
            pltpu.VMEM((6144, 128), F32),
            pltpu.VMEM((64, 3, 2, 16, 128), BF16),
            pltpu.VMEM((10, 3, 2, 128, 128), BF16),
            pltpu.VMEM((2, 8, 3, 128, 128), BF16),
            pltpu.VMEM((3, 2, 64, 128), BF16),
            pltpu.VMEM((3, 4, 64, 128), F32),
            pltpu.VMEM((64, 128), F32),
            pltpu.VMEM((10, 128, 128), F32),
            pltpu.VMEM((4, 2, 8, 128), F32),
            pltpu.VMEM((128, 256), F32),
            pltpu.VMEM((32, 4, 128), F32),
            pltpu.VMEM((32, 4, 128), F32),
            pltpu.VMEM((4, 128), F32),
            pltpu.VMEM((8, 4, 128), F32),
            pltpu.VMEM((4, 128), F32),
            pltpu.VMEM((32, 4, 128), F32),
            dma((3,)), dma((3,)), dma((10,)), dma((10, 3)), dma((2, 8)), dma((2, 8)),
            dma((2,)), dma((2,)), dma((3,)), dma((3,)), dma((2,)),
            pltpu.SemaphoreType.REGULAR((3,)),
        ],
        compiler_params=pltpu.CompilerParams(
            collective_id=0, has_side_effects=True, vmem_limit_bytes=32 << 20
        ),
    )(flow, large, mod_t, metric)


def whiten_kernel(cells, vh, vl, g_ref, out_hbm, out_v, out_sem):
    half = g_ref[...].reshape(128, 128)
    correlation = (half + half.T) / cells
    eye = (
        lax.broadcasted_iota(jnp.int32, (128, 128), 0) == lax.broadcasted_iota(jnp.int32, (128, 128), 1)
    ).astype(F32)
    frob_scale = jnp.sqrt(jnp.sum(correlation * correlation, keepdims=True) + 1e-06)

    def halves(a):
        high = a.astype(BF16)
        return high, (a - high.astype(F32)).astype(BF16)

    def dot(a, b):
        a_high, a_low = halves(a)
        b_high, b_low = halves(b)
        left = jnp.concatenate([a_high, a_high, a_low], axis=1)
        right = jnp.concatenate([b_high, b_low, b_high], axis=0)
        return jnp.dot(left, right, preferred_element_type=F32)

    approx = correlation / frob_scale
    factor = 0.5 * (3.0 * eye - approx)
    approx = dot(approx, factor)
    inverse = factor
    for repeat in range(1, NSITER):
        factor = 0.5 * (3.0 * eye - dot(inverse, approx))
        if repeat < NSITER - 1:
            approx = dot(approx, factor)
        inverse = dot(factor, inverse)
    left = jnp.concatenate(
        [jnp.concatenate([w, w], axis=1) for w in halves(inverse / jnp.sqrt(frob_scale))], axis=0
    )

    stores = []
    for k in range(6):
        right = jnp.concatenate([vh[k], vl[k]], axis=0)
        parts = jnp.dot(left, right, preferred_element_type=F32)
        result = parts[:128] + parts[128:]
        for x in range(8):
            out_v[k, pl.ds(x, 128, stride=8), :] = result[:, 128 * x : 128 * (x + 1)]
        store = pltpu.make_async_copy(
            out_v.at[k].reshape(128, 8, 128), out_hbm.at[:, k // 2, k % 2], out_sem.at[k]
        )
        store.start()
        stores.append(store)
    for store in stores:
        store.wait()


def whiten(vh, vl, gram, cells):
    vmem = pl.BlockSpec(memory_space=pltpu.VMEM)
    return pl.pallas_call(
        functools.partial(whiten_kernel, cells),
        name="whiten",
        out_shape=jax.ShapeDtypeStruct((128, 3, 2, 8, 128), F32),
        in_specs=[vmem, vmem, vmem],
        out_specs=pl.BlockSpec(memory_space=pl.ANY),
        scratch_shapes=[pltpu.VMEM((6, 1024, 128), F32), pltpu.SemaphoreType.DMA((6,))],
        compiler_params=pltpu.CompilerParams(vmem_limit_bytes=32 << 20),
    )(vh, vl, gram)


def per_device(flow, large_scale, modulation, metric):
    sources = (flow.reshape(16, 384, 128), large_scale, modulation.T, metric)
    vh, vl, gram = gather(*(pltpu.with_memory_space_constraint(a, pltpu.HBM) for a in sources))
    return whiten(vh, vl, gram, 3.0 * 64 * 64 * 128)


def solution(mesh):
    return jax.shard_map(
        per_device,
        mesh=mesh,
        in_specs=(
            P("snap", None, "slab", None, None),
            P(None, "slab", None, None),
            P(),
            P(None, "slab", None, None),
        ),
        out_specs=P(None, None, "slab", "snap", None),
        check_vma=False,
    )
```

```python
import functools

import jax
import jax.numpy as jnp
from jax import lax
from jax.experimental import pallas as pl
from jax.experimental.pallas import tpu as pltpu
from jax.sharding import PartitionSpec as P

NSITER = 6
F32 = jnp.float32
BF16 = jnp.bfloat16
MESH = pl.DeviceIdType.MESH


def remote(src, dst, ssem, rsem, dev):
    return pltpu.make_async_remote_copy(
        src_ref=src, dst_ref=dst, send_sem=ssem, recv_sem=rsem, device_id=dev, device_id_type=MESH
    )


def wait_bytes(ref, sem):
    pltpu.make_async_copy(ref, ref, sem).wait()


def gather_kernel(
    flow_hbm, large_hbm, mod_hbm, metric_hbm,
    vh, vl, g_out,
    flow_v, flow_f, send, cols, halo, large_b, large_f, mod_v, mod_b, met,
    acc, gs, rx, zs, rz, ag, gf,
    in_sem, big_sem, xs_sem, xr_sem, hs_sem, hr_sem, ls_sem, lr_sem, as_sem, ar_sem, edge_sem, tokens,
):
    slab = lax.axis_index("slab")
    i = lax.axis_index("snap")
    z = slab // 4
    y = lax.rem(slab, 4)
    up = lax.rem(slab + 1, 32)
    down = lax.rem(slab + 31, 32)

    q = 8 * y + i
    side_dev = [{"slab": down, "snap": i}, {"slab": up, "snap": i}]
    z_side = [{"slab": lax.rem(slab + 4, 32), "snap": i}, {"slab": lax.rem(slab + 28, 32), "snap": i}]
    row_order = (4, 5, 2, 3, 6, 7, 1)
    row_dev = [{"slab": slab, "snap": i ^ d} for d in row_order]
    y_dev = [{"slab": slab ^ d, "snap": i} for d in (2, 1, 3)]
    barrier = pltpu.get_barrier_semaphore()
    cross_dev = [{"slab": down, "snap": i ^ 1}, {"slab": up, "snap": i ^ 1}]
    greeted = row_dev + y_dev + side_dev + cross_dev + z_side
    for dev in greeted:
        pl.semaphore_signal(barrier, inc=1, device_id=dev, device_id_type=MESH)

    flow_in = [
        pltpu.make_async_copy(
            flow_hbm.at[:, pl.ds(128 * c, 128)], flow_v.at[:, pl.ds(128 * c, 128)], big_sem.at[c]
        )
        for c in range(3)
    ]
    for copy in flow_in:
        copy.start()
    large_in = pltpu.make_async_copy(large_hbm, large_b, in_sem.at[0])
    large_in.start()
    mod_in = pltpu.make_async_copy(mod_hbm, mod_v, in_sem.at[1])
    mod_in.start()
    met_in = pltpu.make_async_copy(
        metric_hbm.at[:, :, pl.ds(pl.multiple_of(8 * i, 8), 8), :], met, in_sem.at[2]
    )
    met_in.start()

    def widen(c):
        def one(s, carry):
            for p in range(2):
                for b in range(8):
                    cy = 2 * c + p
                    row = pl.multiple_of((cy * 8 + b) * 128 + 8 * s, 8)
                    flow_f[pl.ds(row, 8), :] = flow_v[s, pl.ds(cy * 64 + 8 * b, 8), :].astype(F32)
            return carry

        lax.fori_loop(0, 16, one, 0)

    def transpose(t, c):
        for b in range(8):
            for p in range(2):
                tile = flow_f[pl.ds(((2 * c + p) * 8 + b) * 128 + t, 16, stride=8), :]
                send[8 * b + t, c, p] = tile.astype(BF16)

    def block(d):
        return pl.ds(16 * d, 16)

    rows8 = pl.ds(pl.multiple_of(8 * i, 8), 8)

    def send_unit(t, c):
        for e in range(2):
            for side in range(2):
                remote(
                    send.at[8 * (i ^ e) + t, c, side], halo.at[1 - side, t, c, block(e)],
                    hs_sem.at[side, t], hr_sem.at[1 - side, t],
                    {"slab": (down, up)[side], "snap": i ^ e},
                ).start()
        for d in row_order:
            target = i ^ d
            remote(
                send.at[8 * target + t, c], cols.at[t + 1, c, :, block(d), :],
                xs_sem.at[t + 1], xr_sem.at[t + 1, c], {"slab": slab, "snap": target},
            ).start()
        pltpu.make_async_copy(
            send.at[8 * i + t, c], cols.at[t + 1, c, :, block(0), :], xr_sem.at[t + 1, c]
        ).start()

    flow_in[0].wait()
    widen(0)
    transpose(0, 0)
    pl.semaphore_wait(barrier, len(greeted))
    for c in (1, 2):
        flow_in[c].wait()
        send_unit(0, c - 1)
        if c == 1:
            for dev in z_side:
                pl.semaphore_signal(tokens.at[0], inc=1, device_id=dev, device_id_type=MESH)
            for dev in side_dev:
                pl.semaphore_signal(tokens.at[3], inc=1, device_id=dev, device_id_type=MESH)
        widen(c)
        transpose(0, c)

    def send_step(u, carry):
        transpose(lax.div(u + 1, 3), lax.rem(u + 1, 3))
        send_unit(lax.div(u, 3), lax.rem(u, 3))
        return carry

    lax.fori_loop(2, 23, send_step, 0)
    send_unit(7, 2)
    pl.semaphore_wait(tokens.at[3], 2)
    for side in range(2):
        for d in row_order[:-1]:
            target = i ^ d
            remote(
                send.at[8 * target + 7, 2, side], halo.at[1 - side, 7, 2, block(d)],
                hs_sem.at[side, 7], hr_sem.at[1 - side, 7],
                {"slab": (down, up)[side], "snap": target},
            ).start()

    def edge_of(k):
        core = lax.rem(k, 2)
        return send.at[lax.rem(8 * k + 63 + 9 * core, 64), pl.ds(1, 2)], 9 * core

    for d in row_order:
        target = i ^ d
        source, slot = edge_of(target)
        remote(
            source, cols.at[slot, pl.ds(1, 2), :, block(d), :],
            edge_sem.at[0], xr_sem.at[slot, 0], {"slab": slab, "snap": target},
        ).start()
    source, slot = edge_of(i)
    pltpu.make_async_copy(
        source, cols.at[slot, pl.ds(1, 2), :, block(0), :], xr_sem.at[slot, 0]
    ).start()
    large_in.wait()
    for c in range(3):
        for p in range(2):
            large_f[c, p + 1] = large_b[c, p].astype(F32)
    pl.semaphore_wait(tokens.at[0], 2)
    for dev in z_side:
        pl.semaphore_signal(tokens.at[1], inc=1, device_id=dev, device_id_type=MESH)
    mod_in.wait()

    def spread(k, carry):
        column = lax.rem(8 * i + k + 63, 64)
        mod_b[k] = jnp.broadcast_to(mod_v[pl.ds(column, 1), :], (128, 128)).T
        return carry

    lax.fori_loop(0, 10, spread, 0)
    large_copies = [
        remote(large_f.at[:, 1, rows8, :], large_f.at[:, 3, rows8, :], ls_sem.at[0], lr_sem.at[0], side_dev[0]),
        remote(large_f.at[:, 2, rows8, :], large_f.at[:, 0, rows8, :], ls_sem.at[1], lr_sem.at[1], side_dev[1]),
    ]
    for copy in large_copies:
        copy.start()

    pl.semaphore_wait(tokens.at[1], 2)
    for dev in z_side:
        pl.semaphore_signal(tokens.at[2], inc=1, device_id=dev, device_id_type=MESH)
    met_in.wait()
    acc[...] = jnp.zeros((128, 256), F32)

    rest = pl.ds(32, 96)

    def pass_on(xx, c):
        wait_bytes(cols.at[xx, c], xr_sem.at[xx, c])

        def forward():
            for side in range(2):
                remote(
                    cols.at[xx, c, side, rest], halo.at[1 - side, xx - 1, c, rest],
                    hs_sem.at[side, xx - 1], hr_sem.at[1 - side, xx - 1], side_dev[side],
                ).start()

        if c < 2:
            forward()
        else:
            pl.when(xx < 8)(forward)

    def pass_step(k, carry):
        for c in range(3):
            pass_on(k + 1, c)
        return carry

    lax.fori_loop(0, 3, pass_step, 0)
    for copy in large_copies:
        copy.wait()

    @pl.when(slab == 0)
    def _():
        large_f[:, 0] = jnp.zeros((3, 64, 128), F32)

    @pl.when(slab == 31)
    def _():
        large_f[:, 3] = jnp.zeros((3, 64, 128), F32)


    def column(k, carry):
        xx = k + 2 - 7 * lax.div(k, 6) + 6 * lax.div(k, 7)

        @pl.when(k < 5)
        def _():
            for c in range(3):
                pass_on(k + 4, c)

        @pl.when(k == 6)
        def _():
            wait_bytes(cols.at[0, pl.ds(1, 2)], xr_sem.at[0, 0])

        @pl.when(k == 7)
        def _():
            wait_bytes(cols.at[9, pl.ds(1, 2)], xr_sem.at[9, 0])

        for side in range(2):
            wait_bytes(halo.at[side, xx - 1], hr_sem.at[side, xx - 1])

        @pl.when(slab == 0)
        def _():
            halo[0, xx - 1] = jnp.zeros((3, 128, 128), BF16)

        @pl.when(slab == 31)
        def _():
            halo[1, xx - 1] = jnp.zeros((3, 128, 128), BF16)

        here = 8 * i + xx - 1
        before = lax.rem(here + 63, 64)
        after = lax.rem(here + 1, 64)
        base = [[large_f[c, p, pl.ds(here, 1), :] for p in range(4)] for c in range(3)]
        base_m = [[large_f[c, p + 1, pl.ds(before, 1), :] for p in range(2)] for c in (1, 2)]
        base_p = [[large_f[c, p + 1, pl.ds(after, 1), :] for p in range(2)] for c in (1, 2)]
        half = [[0.5 * met[m, p, pl.ds(xx - 1, 1), :] for p in range(2)] for m in range(4)]
        lanes = pl.ds(pl.multiple_of(128 * (xx - 1), 128), 128)

        def snaps(s, inner):
            r = pl.ds(pl.multiple_of(16 * s, 16), 16)
            own = pl.ds(pl.multiple_of(16 * (s ^ i), 16), 16)
            m0 = mod_b[xx, own, :]
            mm = mod_b[xx - 1, own, :]
            mp = mod_b[xx + 1, own, :]

            def field(c):
                return [
                    halo[0, xx - 1, c, r, :].astype(F32) + m0 * base[c][0],
                    cols[xx, c, 0, r, :].astype(F32) + m0 * base[c][1],
                    cols[xx, c, 1, r, :].astype(F32) + m0 * base[c][2],
                    halo[1, xx - 1, c, r, :].astype(F32) + m0 * base[c][3],
                ]

            def along_x(c, p):
                right = cols[xx + 1, c, p, r, :].astype(F32) + mp * base_p[c - 1][p]
                left = cols[xx - 1, c, p, r, :].astype(F32) + mm * base_m[c - 1][p]
                return right - left

            def along_z(f):
                return pltpu.roll(f, 127, 1) - pltpu.roll(f, 1, 1)

            u, v, w = field(0), field(1), field(2)
            for p in range(2):
                gx, sxy, gy, gz = (half[m][p] for m in range(4))
                du = u[p + 2] - u[p]
                dv = v[p + 2] - v[p]
                dw = w[p + 2] - w[p]
                around = (
                    gy * dw - gz * along_z(v[p + 1]),
                    gz * along_z(u[p + 1]) - (gx * along_x(2, p) + sxy * dw),
                    (gx * along_x(1, p) + sxy * dv) - gy * du,
                )
                for c in range(3):
                    high = around[c].astype(BF16)
                    vh[2 * c + p, own, lanes] = high
                    vl[2 * c + p, own, lanes] = (around[c] - high.astype(F32)).astype(BF16)
            return inner

        lax.fori_loop(0, 8, snaps, 0, unroll=4)

        @pl.when(k == 4)
        def _():
            core = lax.rem(i, 2)
            for b in range(8):
                remote(
                    cols.at[8 - 7 * core, pl.ds(1, 2), :, block(b), :],
                    cols.at[9 * core, pl.ds(1, 2), :, block(b ^ 1), :],
                    edge_sem.at[1], xr_sem.at[9 * core, 0], {"slab": slab, "snap": i ^ 1},
                ).start()

        rows_h = jnp.concatenate([vh[cy, :, lanes] for cy in range(6)], axis=1)
        rows_l = jnp.concatenate([vl[cy, :, lanes] for cy in range(6)], axis=1)
        both = jnp.concatenate([rows_h, rows_l], axis=0)
        acc[...] += lax.dot_general(
            rows_h, both, (((1,), (1,)), ((), ())), preferred_element_type=F32
        )
        return carry

    lax.fori_loop(0, 8, column, 0)
    half_gram = 0.5 * acc[:, :128] + acc[:, 128:]
    for k in range(32):
        gs[k] = half_gram[4 * k : 4 * k + 4, :]

    plane_order = sorted(range(1, 32), key=lambda d: -(2 * ((d >> 4) & 1) + 2 * ((d >> 2) & 1) + ((d >> 3) & 1) + ((d >> 1) & 1)))
    plane = [(q ^ d, {"slab": slab ^ (d >> 3), "snap": i ^ (d & 7)}) for d in plane_order]
    line = [(z ^ d, {"slab": slab ^ (4 * d), "snap": i}) for d in (4, 5, 3, 7, 6, 2, 1)]

    def exchange(stage, mine, partners, src_of, dst, drain):
        for target, dev in partners:
            remote(src_of(target), dst.at[mine], as_sem.at[stage], ar_sem.at[stage], dev).start()
        pltpu.make_async_copy(src_of(mine), dst.at[mine], ar_sem.at[stage]).start()
        drain()
        wait_bytes(dst, ar_sem.at[stage])

    def drain_columns():
        for t in range(8):
            wait_bytes(send.at[pl.ds(0, 7)], xs_sem.at[t + 1])
        wait_bytes(send.at[pl.ds(0, 7), pl.ds(1, 2)], edge_sem.at[0])
        wait_bytes(cols.at[0, pl.ds(1, 2)], edge_sem.at[1])
        for side in range(2):
            for k in range(8):
                wait_bytes(cols.at[k + 1, :, side], hs_sem.at[side, k])

    pl.semaphore_wait(tokens.at[2], 2)
    exchange(0, q, plane, lambda k: gs.at[k], rx, drain_columns)
    zs[...] = jnp.sum(rx[...], axis=0)
    exchange(1, z, line, lambda k: zs, rz, lambda: wait_bytes(rx.at[pl.ds(0, 31)], as_sem.at[0]))
    ag[...] = jnp.sum(rz[...], axis=0)
    exchange(2, q, plane, lambda k: ag, g_out, lambda: wait_bytes(rz.at[pl.ds(0, 7)], as_sem.at[1]))
    wait_bytes(g_out.at[pl.ds(0, 31)], as_sem.at[2])


def gather(flow, large, mod_t, metric):
    vmem = pl.BlockSpec(memory_space=pltpu.VMEM)
    dma = pltpu.SemaphoreType.DMA
    return pl.pallas_call(
        gather_kernel,
        name="gather",
        out_shape=(
            pltpu.VMEM((6, 128, 1024), BF16),
            pltpu.VMEM((6, 128, 1024), BF16),
            pltpu.VMEM((32, 4, 128), F32),
        ),
        in_specs=[pl.BlockSpec(memory_space=pltpu.HBM)] * 4,
        out_specs=(vmem, vmem, vmem),
        scratch_shapes=[
            pltpu.VMEM((16, 384, 128), BF16),
            pltpu.VMEM((6144, 128), F32),
            pltpu.VMEM((64, 3, 2, 16, 128), BF16),
            pltpu.VMEM((10, 3, 2, 128, 128), BF16),
            pltpu.VMEM((2, 8, 3, 128, 128), BF16),
            pltpu.VMEM((3, 2, 64, 128), BF16),
            pltpu.VMEM((3, 4, 64, 128), F32),
            pltpu.VMEM((64, 128), F32),
            pltpu.VMEM((10, 128, 128), F32),
            pltpu.VMEM((4, 2, 8, 128), F32),
            pltpu.VMEM((128, 256), F32),
            pltpu.VMEM((32, 4, 128), F32),
            pltpu.VMEM((32, 4, 128), F32),
            pltpu.VMEM((4, 128), F32),
            pltpu.VMEM((8, 4, 128), F32),
            pltpu.VMEM((4, 128), F32),
            pltpu.VMEM((32, 4, 128), F32),
            dma((3,)), dma((3,)), dma((10,)), dma((10, 3)), dma((2, 8)), dma((2, 8)),
            dma((2,)), dma((2,)), dma((3,)), dma((3,)), dma((2,)),
            pltpu.SemaphoreType.REGULAR((4,)),
        ],
        compiler_params=pltpu.CompilerParams(
            collective_id=0, has_side_effects=True, vmem_limit_bytes=32 << 20
        ),
    )(flow, large, mod_t, metric)


def whiten_kernel(cells, vh, vl, g_ref, out_hbm, out_v, out_sem):
    half = g_ref[...].reshape(128, 128)
    correlation = (half + half.T) / cells
    eye = (
        lax.broadcasted_iota(jnp.int32, (128, 128), 0) == lax.broadcasted_iota(jnp.int32, (128, 128), 1)
    ).astype(F32)
    frob_scale = jnp.sqrt(jnp.sum(correlation * correlation, keepdims=True) + 1e-06)

    def halves(a):
        high = a.astype(BF16)
        return high, (a - high.astype(F32)).astype(BF16)

    def dot(a, b):
        a_high, a_low = halves(a)
        b_high, b_low = halves(b)
        left = jnp.concatenate([a_high, a_high, a_low], axis=1)
        right = jnp.concatenate([b_high, b_low, b_high], axis=0)
        return jnp.dot(left, right, preferred_element_type=F32)

    approx = correlation / frob_scale
    factor = 0.5 * (3.0 * eye - approx)
    approx = dot(approx, factor)
    inverse = factor
    for repeat in range(1, NSITER):
        factor = 0.5 * (3.0 * eye - dot(inverse, approx))
        if repeat < NSITER - 1:
            approx = dot(approx, factor)
        inverse = dot(factor, inverse)
    left = jnp.concatenate(
        [jnp.concatenate([w, w], axis=1) for w in halves(inverse / jnp.sqrt(frob_scale))], axis=0
    )

    stores = []
    for k in range(6):
        right = jnp.concatenate([vh[k], vl[k]], axis=0)
        parts = jnp.dot(left, right, preferred_element_type=F32)
        result = parts[:128] + parts[128:]
        for x in range(8):
            out_v[k, pl.ds(x, 128, stride=8), :] = result[:, 128 * x : 128 * (x + 1)]
        store = pltpu.make_async_copy(
            out_v.at[k].reshape(128, 8, 128), out_hbm.at[:, k // 2, k % 2], out_sem.at[k]
        )
        store.start()
        stores.append(store)
    for store in stores:
        store.wait()


def whiten(vh, vl, gram, cells):
    vmem = pl.BlockSpec(memory_space=pltpu.VMEM)
    return pl.pallas_call(
        functools.partial(whiten_kernel, cells),
        name="whiten",
        out_shape=jax.ShapeDtypeStruct((128, 3, 2, 8, 128), F32),
        in_specs=[vmem, vmem, vmem],
        out_specs=pl.BlockSpec(memory_space=pl.ANY),
        scratch_shapes=[pltpu.VMEM((6, 1024, 128), F32), pltpu.SemaphoreType.DMA((6,))],
        compiler_params=pltpu.CompilerParams(vmem_limit_bytes=32 << 20),
    )(vh, vl, gram)


def per_device(flow, large_scale, modulation, metric):
    sources = (flow.reshape(16, 384, 128), large_scale, modulation.T, metric)
    vh, vl, gram = gather(*(pltpu.with_memory_space_constraint(a, pltpu.HBM) for a in sources))
    return whiten(vh, vl, gram, 3.0 * 64 * 64 * 128)


def solution(mesh):
    return jax.shard_map(
        per_device,
        mesh=mesh,
        in_specs=(
            P("snap", None, "slab", None, None),
            P(None, "slab", None, None),
            P(),
            P(None, "slab", None, None),
        ),
        out_specs=P(None, None, "slab", "snap", None),
        check_vma=False,
    )
```

```python
import functools

import jax
import jax.numpy as jnp
from jax import lax
from jax.experimental import pallas as pl
from jax.experimental.pallas import tpu as pltpu
from jax.sharding import PartitionSpec as P

NSITER = 6
F32 = jnp.float32
BF16 = jnp.bfloat16
MESH = pl.DeviceIdType.MESH


def remote(src, dst, ssem, rsem, dev):
    return pltpu.make_async_remote_copy(
        src_ref=src, dst_ref=dst, send_sem=ssem, recv_sem=rsem, device_id=dev, device_id_type=MESH
    )


def wait_bytes(ref, sem):
    pltpu.make_async_copy(ref, ref, sem).wait()


def gather_kernel(
    flow_hbm, large_hbm, mod_hbm, metric_hbm,
    vh, vl, g_out,
    flow_v, flow_f, send, cols, halo, large_b, large_f, mod_v, mod_b, met,
    acc, gs, rx, zs, rz, ag, gf,
    in_sem, big_sem, xs_sem, xr_sem, hs_sem, hr_sem, ls_sem, lr_sem, as_sem, ar_sem, edge_sem, tokens,
):
    slab = lax.axis_index("slab")
    i = lax.axis_index("snap")
    z = slab // 4
    y = lax.rem(slab, 4)
    up = lax.rem(slab + 1, 32)
    down = lax.rem(slab + 31, 32)

    q = 8 * y + i
    side_dev = [{"slab": down, "snap": i}, {"slab": up, "snap": i}]
    z_side = [{"slab": lax.rem(slab + 4, 32), "snap": i}, {"slab": lax.rem(slab + 28, 32), "snap": i}]
    row_order = (4, 5, 2, 3, 6, 7, 1)
    row_dev = [{"slab": slab, "snap": i ^ d} for d in row_order]
    y_dev = [{"slab": slab ^ d, "snap": i} for d in (2, 1, 3)]
    barrier = pltpu.get_barrier_semaphore()
    cross_dev = [{"slab": down, "snap": i ^ 1}, {"slab": up, "snap": i ^ 1}]
    greeted = row_dev + y_dev + side_dev + cross_dev + z_side
    for dev in greeted:
        pl.semaphore_signal(barrier, inc=1, device_id=dev, device_id_type=MESH)

    flow_in = [
        pltpu.make_async_copy(
            flow_hbm.at[:, pl.ds(128 * c, 128)], flow_v.at[:, pl.ds(128 * c, 128)], big_sem.at[c]
        )
        for c in range(3)
    ]
    for copy in flow_in:
        copy.start()
    large_in = pltpu.make_async_copy(large_hbm, large_b, in_sem.at[0])
    large_in.start()
    mod_in = pltpu.make_async_copy(mod_hbm, mod_v, in_sem.at[1])
    mod_in.start()
    met_in = pltpu.make_async_copy(
        metric_hbm.at[:, :, pl.ds(pl.multiple_of(8 * i, 8), 8), :], met, in_sem.at[2]
    )
    met_in.start()

    def widen(c):
        def one(s, carry):
            for p in range(2):
                for b in range(8):
                    cy = 2 * c + p
                    row = pl.multiple_of((cy * 8 + b) * 128 + 8 * s, 8)
                    flow_f[pl.ds(row, 8), :] = flow_v[s, pl.ds(cy * 64 + 8 * b, 8), :].astype(F32)
            return carry

        lax.fori_loop(0, 16, one, 0)

    def transpose(t, c):
        for b in range(8):
            for p in range(2):
                tile = flow_f[pl.ds(((2 * c + p) * 8 + b) * 128 + t, 16, stride=8), :]
                send[8 * b + t, c, p] = tile.astype(BF16)

    def block(d):
        return pl.ds(16 * d, 16)

    rows8 = pl.ds(pl.multiple_of(8 * i, 8), 8)

    def send_unit(t, c):
        for e in range(2):
            for side in range(2):
                remote(
                    send.at[8 * (i ^ e) + t, c, side], halo.at[1 - side, t, c, block(e)],
                    hs_sem.at[side, t], hr_sem.at[1 - side, t],
                    {"slab": (down, up)[side], "snap": i ^ e},
                ).start()
        for d in row_order:
            target = i ^ d
            remote(
                send.at[8 * target + t, c], cols.at[t + 1, c, :, block(d), :],
                xs_sem.at[t + 1], xr_sem.at[t + 1, c], {"slab": slab, "snap": target},
            ).start()
        pltpu.make_async_copy(
            send.at[8 * i + t, c], cols.at[t + 1, c, :, block(0), :], xr_sem.at[t + 1, c]
        ).start()

    flow_in[0].wait()
    widen(0)
    transpose(0, 0)
    pl.semaphore_wait(barrier, len(greeted))
    for c in (1, 2):
        flow_in[c].wait()
        send_unit(0, c - 1)
        if c == 1:
            for dev in z_side:
                pl.semaphore_signal(tokens.at[0], inc=1, device_id=dev, device_id_type=MESH)
            for dev in side_dev:
                pl.semaphore_signal(tokens.at[3], inc=1, device_id=dev, device_id_type=MESH)
        widen(c)
        transpose(0, c)

    def send_step(u, carry):
        transpose(lax.div(u + 1, 3), lax.rem(u + 1, 3))
        send_unit(lax.div(u, 3), lax.rem(u, 3))
        return carry

    lax.fori_loop(2, 23, send_step, 0)
    send_unit(7, 2)
    pl.semaphore_wait(tokens.at[3], 2)
    for side in range(2):
        for d in row_order[:-1]:
            target = i ^ d
            remote(
                send.at[8 * target + 7, 2, side], halo.at[1 - side, 7, 2, block(d)],
                hs_sem.at[side, 7], hr_sem.at[1 - side, 7],
                {"slab": (down, up)[side], "snap": target},
            ).start()

    def edge_of(k):
        core = lax.rem(k, 2)
        return send.at[lax.rem(8 * k + 63 + 9 * core, 64), pl.ds(1, 2)], 9 * core

    for d in row_order:
        target = i ^ d
        source, slot = edge_of(target)
        remote(
            source, cols.at[slot, pl.ds(1, 2), :, block(d), :],
            edge_sem.at[0], xr_sem.at[slot, 0], {"slab": slab, "snap": target},
        ).start()
    source, slot = edge_of(i)
    pltpu.make_async_copy(
        source, cols.at[slot, pl.ds(1, 2), :, block(0), :], xr_sem.at[slot, 0]
    ).start()
    large_in.wait()
    for c in range(3):
        for p in range(2):
            large_f[c, p + 1] = large_b[c, p].astype(F32)
    pl.semaphore_wait(tokens.at[0], 2)
    for dev in z_side:
        pl.semaphore_signal(tokens.at[1], inc=1, device_id=dev, device_id_type=MESH)
    mod_in.wait()

    def spread(k, carry):
        column = lax.rem(8 * i + k + 63, 64)
        mod_b[k] = jnp.broadcast_to(mod_v[pl.ds(column, 1), :], (128, 128)).T
        return carry

    lax.fori_loop(0, 10, spread, 0)
    large_copies = [
        remote(large_f.at[:, 1, rows8, :], large_f.at[:, 3, rows8, :], ls_sem.at[0], lr_sem.at[0], side_dev[0]),
        remote(large_f.at[:, 2, rows8, :], large_f.at[:, 0, rows8, :], ls_sem.at[1], lr_sem.at[1], side_dev[1]),
    ]
    for copy in large_copies:
        copy.start()

    pl.semaphore_wait(tokens.at[1], 2)
    for dev in z_side:
        pl.semaphore_signal(tokens.at[2], inc=1, device_id=dev, device_id_type=MESH)
    met_in.wait()
    acc[...] = jnp.zeros((128, 256), F32)

    rest = pl.ds(32, 96)

    def pass_on(xx, c):
        wait_bytes(cols.at[xx, c], xr_sem.at[xx, c])

        def forward():
            for side in range(2):
                remote(
                    cols.at[xx, c, side, rest], halo.at[1 - side, xx - 1, c, rest],
                    hs_sem.at[side, xx - 1], hr_sem.at[1 - side, xx - 1], side_dev[side],
                ).start()

        if c < 2:
            forward()
        else:
            pl.when(xx < 8)(forward)

    def pass_step(k, carry):
        for c in range(3):
            pass_on(k + 1, c)
        return carry

    lax.fori_loop(0, 4, pass_step, 0)
    for copy in large_copies:
        copy.wait()

    @pl.when(slab == 0)
    def _():
        large_f[:, 0] = jnp.zeros((3, 64, 128), F32)

    @pl.when(slab == 31)
    def _():
        large_f[:, 3] = jnp.zeros((3, 64, 128), F32)


    def column(k, carry):
        xx = k + 2 - 7 * lax.div(k, 6) + 6 * lax.div(k, 7)

        @pl.when(k < 4)
        def _():
            for c in range(3):
                pass_on(k + 5, c)

        @pl.when(k == 6)
        def _():
            wait_bytes(cols.at[0, pl.ds(1, 2)], xr_sem.at[0, 0])

        @pl.when(k == 7)
        def _():
            wait_bytes(cols.at[9, pl.ds(1, 2)], xr_sem.at[9, 0])

        for side in range(2):
            wait_bytes(halo.at[side, xx - 1], hr_sem.at[side, xx - 1])

        @pl.when(slab == 0)
        def _():
            halo[0, xx - 1] = jnp.zeros((3, 128, 128), BF16)

        @pl.when(slab == 31)
        def _():
            halo[1, xx - 1] = jnp.zeros((3, 128, 128), BF16)

        here = 8 * i + xx - 1
        before = lax.rem(here + 63, 64)
        after = lax.rem(here + 1, 64)
        base = [[large_f[c, p, pl.ds(here, 1), :] for p in range(4)] for c in range(3)]
        base_m = [[large_f[c, p + 1, pl.ds(before, 1), :] for p in range(2)] for c in (1, 2)]
        base_p = [[large_f[c, p + 1, pl.ds(after, 1), :] for p in range(2)] for c in (1, 2)]
        half = [[0.5 * met[m, p, pl.ds(xx - 1, 1), :] for p in range(2)] for m in range(4)]
        lanes = pl.ds(pl.multiple_of(128 * (xx - 1), 128), 128)

        def snaps(s, inner):
            r = pl.ds(pl.multiple_of(16 * s, 16), 16)
            own = pl.ds(pl.multiple_of(16 * (s ^ i), 16), 16)
            m0 = mod_b[xx, own, :]
            mm = mod_b[xx - 1, own, :]
            mp = mod_b[xx + 1, own, :]

            def field(c):
                return [
                    halo[0, xx - 1, c, r, :].astype(F32) + m0 * base[c][0],
                    cols[xx, c, 0, r, :].astype(F32) + m0 * base[c][1],
                    cols[xx, c, 1, r, :].astype(F32) + m0 * base[c][2],
                    halo[1, xx - 1, c, r, :].astype(F32) + m0 * base[c][3],
                ]

            def along_x(c, p):
                right = cols[xx + 1, c, p, r, :].astype(F32) + mp * base_p[c - 1][p]
                left = cols[xx - 1, c, p, r, :].astype(F32) + mm * base_m[c - 1][p]
                return right - left

            def along_z(f):
                return pltpu.roll(f, 127, 1) - pltpu.roll(f, 1, 1)

            u, v, w = field(0), field(1), field(2)
            for p in range(2):
                gx, sxy, gy, gz = (half[m][p] for m in range(4))
                du = u[p + 2] - u[p]
                dv = v[p + 2] - v[p]
                dw = w[p + 2] - w[p]
                around = (
                    gy * dw - gz * along_z(v[p + 1]),
                    gz * along_z(u[p + 1]) - (gx * along_x(2, p) + sxy * dw),
                    (gx * along_x(1, p) + sxy * dv) - gy * du,
                )
                for c in range(3):
                    high = around[c].astype(BF16)
                    vh[2 * c + p, own, lanes] = high
                    vl[2 * c + p, own, lanes] = (around[c] - high.astype(F32)).astype(BF16)
            return inner

        lax.fori_loop(0, 8, snaps, 0, unroll=4)

        @pl.when(k == 3)
        def _():
            core = lax.rem(i, 2)
            for b in range(8):
                remote(
                    cols.at[8 - 7 * core, pl.ds(1, 2), :, block(b), :],
                    cols.at[9 * core, pl.ds(1, 2), :, block(b ^ 1), :],
                    edge_sem.at[1], xr_sem.at[9 * core, 0], {"slab": slab, "snap": i ^ 1},
                ).start()

        rows_h = jnp.concatenate([vh[cy, :, lanes] for cy in range(6)], axis=1)
        rows_l = jnp.concatenate([vl[cy, :, lanes] for cy in range(6)], axis=1)
        both = jnp.concatenate([rows_h, rows_l], axis=0)
        acc[...] += lax.dot_general(
            rows_h, both, (((1,), (1,)), ((), ())), preferred_element_type=F32
        )
        return carry

    lax.fori_loop(0, 8, column, 0)
    half_gram = 0.5 * acc[:, :128] + acc[:, 128:]
    for k in range(32):
        gs[k] = half_gram[4 * k : 4 * k + 4, :]

    plane_order = sorted(range(1, 32), key=lambda d: -(2 * ((d >> 4) & 1) + 2 * ((d >> 2) & 1) + ((d >> 3) & 1) + ((d >> 1) & 1)))
    plane = [(q ^ d, {"slab": slab ^ (d >> 3), "snap": i ^ (d & 7)}) for d in plane_order]
    line = [(z ^ d, {"slab": slab ^ (4 * d), "snap": i}) for d in (4, 5, 3, 7, 6, 2, 1)]

    def exchange(stage, mine, partners, src_of, dst, drain):
        for target, dev in partners:
            remote(src_of(target), dst.at[mine], as_sem.at[stage], ar_sem.at[stage], dev).start()
        pltpu.make_async_copy(src_of(mine), dst.at[mine], ar_sem.at[stage]).start()
        drain()
        wait_bytes(dst, ar_sem.at[stage])

    def drain_columns():
        for t in range(8):
            wait_bytes(send.at[pl.ds(0, 7)], xs_sem.at[t + 1])
        wait_bytes(send.at[pl.ds(0, 7), pl.ds(1, 2)], edge_sem.at[0])
        wait_bytes(cols.at[0, pl.ds(1, 2)], edge_sem.at[1])
        for side in range(2):
            for k in range(8):
                wait_bytes(cols.at[k + 1, :, side], hs_sem.at[side, k])

    pl.semaphore_wait(tokens.at[2], 2)
    exchange(0, q, plane, lambda k: gs.at[k], rx, drain_columns)
    zs[...] = jnp.sum(rx[...], axis=0)
    exchange(1, z, line, lambda k: zs, rz, lambda: wait_bytes(rx.at[pl.ds(0, 31)], as_sem.at[0]))
    ag[...] = jnp.sum(rz[...], axis=0)
    exchange(2, q, plane, lambda k: ag, g_out, lambda: wait_bytes(rz.at[pl.ds(0, 7)], as_sem.at[1]))
    wait_bytes(g_out.at[pl.ds(0, 31)], as_sem.at[2])


def gather(flow, large, mod_t, metric):
    vmem = pl.BlockSpec(memory_space=pltpu.VMEM)
    dma = pltpu.SemaphoreType.DMA
    return pl.pallas_call(
        gather_kernel,
        name="gather",
        out_shape=(
            pltpu.VMEM((6, 128, 1024), BF16),
            pltpu.VMEM((6, 128, 1024), BF16),
            pltpu.VMEM((32, 4, 128), F32),
        ),
        in_specs=[pl.BlockSpec(memory_space=pltpu.HBM)] * 4,
        out_specs=(vmem, vmem, vmem),
        scratch_shapes=[
            pltpu.VMEM((16, 384, 128), BF16),
            pltpu.VMEM((6144, 128), F32),
            pltpu.VMEM((64, 3, 2, 16, 128), BF16),
            pltpu.VMEM((10, 3, 2, 128, 128), BF16),
            pltpu.VMEM((2, 8, 3, 128, 128), BF16),
            pltpu.VMEM((3, 2, 64, 128), BF16),
            pltpu.VMEM((3, 4, 64, 128), F32),
            pltpu.VMEM((64, 128), F32),
            pltpu.VMEM((10, 128, 128), F32),
            pltpu.VMEM((4, 2, 8, 128), F32),
            pltpu.VMEM((128, 256), F32),
            pltpu.VMEM((32, 4, 128), F32),
            pltpu.VMEM((32, 4, 128), F32),
            pltpu.VMEM((4, 128), F32),
            pltpu.VMEM((8, 4, 128), F32),
            pltpu.VMEM((4, 128), F32),
            pltpu.VMEM((32, 4, 128), F32),
            dma((3,)), dma((3,)), dma((10,)), dma((10, 3)), dma((2, 8)), dma((2, 8)),
            dma((2,)), dma((2,)), dma((3,)), dma((3,)), dma((2,)),
            pltpu.SemaphoreType.REGULAR((4,)),
        ],
        compiler_params=pltpu.CompilerParams(
            collective_id=0, has_side_effects=True, vmem_limit_bytes=32 << 20
        ),
    )(flow, large, mod_t, metric)


def whiten_kernel(cells, vh, vl, g_ref, out_hbm, out_v, out_sem):
    half = g_ref[...].reshape(128, 128)
    correlation = (half + half.T) / cells
    eye = (
        lax.broadcasted_iota(jnp.int32, (128, 128), 0) == lax.broadcasted_iota(jnp.int32, (128, 128), 1)
    ).astype(F32)
    frob_scale = jnp.sqrt(jnp.sum(correlation * correlation, keepdims=True) + 1e-06)

    def halves(a):
        high = a.astype(BF16)
        return high, (a - high.astype(F32)).astype(BF16)

    def dot(a, b):
        a_high, a_low = halves(a)
        b_high, b_low = halves(b)
        left = jnp.concatenate([a_high, a_high, a_low], axis=1)
        right = jnp.concatenate([b_high, b_low, b_high], axis=0)
        return jnp.dot(left, right, preferred_element_type=F32)

    approx = correlation / frob_scale
    factor = 0.5 * (3.0 * eye - approx)
    approx = dot(approx, factor)
    inverse = factor
    for repeat in range(1, NSITER):
        factor = 0.5 * (3.0 * eye - dot(inverse, approx))
        if repeat < NSITER - 1:
            approx = dot(approx, factor)
        inverse = dot(factor, inverse)
    left = jnp.concatenate(
        [jnp.concatenate([w, w], axis=1) for w in halves(inverse / jnp.sqrt(frob_scale))], axis=0
    )

    stores = []
    for k in range(6):
        right = jnp.concatenate([vh[k], vl[k]], axis=0)
        parts = jnp.dot(left, right, preferred_element_type=F32)
        result = parts[:128] + parts[128:]
        for x in range(8):
            out_v[k, pl.ds(x, 128, stride=8), :] = result[:, 128 * x : 128 * (x + 1)]
        store = pltpu.make_async_copy(
            out_v.at[k].reshape(128, 8, 128), out_hbm.at[:, k // 2, k % 2], out_sem.at[k]
        )
        store.start()
        stores.append(store)
    for store in stores:
        store.wait()


def whiten(vh, vl, gram, cells):
    vmem = pl.BlockSpec(memory_space=pltpu.VMEM)
    return pl.pallas_call(
        functools.partial(whiten_kernel, cells),
        name="whiten",
        out_shape=jax.ShapeDtypeStruct((128, 3, 2, 8, 128), F32),
        in_specs=[vmem, vmem, vmem],
        out_specs=pl.BlockSpec(memory_space=pl.ANY),
        scratch_shapes=[pltpu.VMEM((6, 1024, 128), F32), pltpu.SemaphoreType.DMA((6,))],
        compiler_params=pltpu.CompilerParams(vmem_limit_bytes=32 << 20),
    )(vh, vl, gram)


def per_device(flow, large_scale, modulation, metric):
    sources = (flow.reshape(16, 384, 128), large_scale, modulation.T, metric)
    vh, vl, gram = gather(*(pltpu.with_memory_space_constraint(a, pltpu.HBM) for a in sources))
    return whiten(vh, vl, gram, 3.0 * 64 * 64 * 128)


def solution(mesh):
    return jax.shard_map(
        per_device,
        mesh=mesh,
        in_specs=(
            P("snap", None, "slab", None, None),
            P(None, "slab", None, None),
            P(),
            P(None, "slab", None, None),
        ),
        out_specs=P(None, None, "slab", "snap", None),
        check_vma=False,
    )
```
